32 devices in a mesh: seq: 8 (over z, x), head: 4 (over y, core).
Axes of the slice: x: 2, y: 2, z: 4, core: 2. Of those that a mesh axis runs over, the one named last changes fastest.
Arguments:
- x_in: bfloat16 [2048, 5120], P('seq', 'head'), may hold values from -6 to 6
- bc_in: bfloat16 [2048, 256], P('seq'), may hold values from -6 to 6
- z_in: bfloat16 [2048, 5120], P('seq', 'head'), may hold values from -6 to 6
- dt_raw: float32 [80, 2048], P('head', 'seq'), may hold values from -3 to 3
- dt_bias: float32 [80], P('head'), may hold values from -2.8 to -1.7
- a_log: float32 [80], P('head'), as said below
- conv_x: float32 [4, 5120], P(None, 'head'), may hold values from -3 to 3
- conv_bc: float32 [4, 256], replicated, may hold values from -3 to 3
- conv_x_bias: float32 [5120], P('head'), may hold values from -3 to 3
- conv_bc_bias: float32 [256], replicated, may hold values from -3 to 3
- norm_weight: float32 [5120], P('head'), may hold values from 0.1 to 1.9
Outputs:
- y_out: bfloat16 [2048, 5120], P('seq', 'head')
The draws below stay inside these ranges and needn't reach their ends.
Inputs may be any that keep to these rules, and one draw needn't show every extreme that they name: a_log is at least log(2 / 2048) and at most 0.
All inputs are finite; a program needn't handle non-finite values.
Results may differ from the reference program's by a relative error of at most 0.012.
Values may be sent and summed in bfloat16 or wider, within the bound.
No kernel may reach another device: no remote copies, remote signals or barrier semaphores. Data moves between devices by JAX's collectives and lax.ppermute only.
A program may use at most 128 MiB of HBM per device.

```python
import jax
import jax.numpy as jnp
from jax import lax

HEADS = 80
HEADDIM = 64
STATE = 128
CONV = 4
SPAN = 256
SEQLEN = 2048
INNER = 5120


def draw_a_log(key, part):
    key_slow = jax.random.fold_in(key, 11)
    key_fast = jax.random.fold_in(key, 12)
    key_pick = jax.random.fold_in(key, 13)
    slow_rates = jax.random.uniform(key_slow, (HEADS,), jnp.float32, jnp.log(2.0 / SEQLEN), jnp.log(8.0 / SEQLEN))
    fast_rates = jax.random.uniform(key_fast, (HEADS,), jnp.float32, jnp.log(0.3), 0.0)
    chosen = jax.random.randint(key_pick, (HEADS,), 0, 10)
    picked = chosen < 5
    return jnp.where(picked, fast_rates, slow_rates)


def level_of(own_key, shape, split, smallest, top_value):
    loudness, own = 1.0, jax.random.fold_in(own_key, 6)
    for axis_at, parts in split:
        heights = jnp.exp(jax.random.uniform(jax.random.fold_in(own, axis_at), (parts,), jnp.float32, smallest / len(split), top_value / len(split)))
        loudness = loudness * jnp.repeat(heights, shape[axis_at] // parts).reshape([-1 if axis == axis_at else 1 for axis in range(len(shape))])
    return loudness


def scatter_about(stream_key, dims, width, bound, cuts=(), dtype=jnp.bfloat16):
    factor_of = level_of(stream_key, dims, cuts, -0.22, 0.18) if cuts else 1.0
    array = jax.random.normal(stream_key, dims, jnp.float32) * width * factor_of
    return jnp.minimum(jnp.maximum(array, -bound), bound).astype(dtype)


def setup_inputs(seed: int = 0) -> dict:
    splits = jax.random.split(jax.random.key(seed), 12)
    x_in = scatter_about(splits[0], (SEQLEN, INNER), 1.0, 6.0, ((0, 8), (1, 4)))
    bc_in = scatter_about(splits[1], (SEQLEN, 2 * STATE), 1.0, 6.0, ((0, 8),))
    z_in = scatter_about(splits[2], (SEQLEN, INNER), 1.0, 6.0, ((0, 8), (1, 4)))
    dt_raw = scatter_about(splits[3], (HEADS, SEQLEN), 0.5, 3.0, ((0, 4), (1, 8)), jnp.float32)
    dt_bias = jnp.clip(-2.8 + 1.0999999 * jax.random.uniform(splits[4], (HEADS,), jnp.float32) ** level_of(splits[4], (HEADS,), ((0, 4),), -0.2, 0.2), -2.8, -1.7)
    a_log = draw_a_log(jax.random.fold_in(splits[11], 71), 0)
    conv_x = scatter_about(splits[6], (CONV, INNER), CONV ** -0.5, 3.0, ((1, 4),), jnp.float32)
    conv_bc = scatter_about(splits[7], (CONV, 2 * STATE), CONV ** -0.5, 3.0, (), jnp.float32)
    conv_x_bias = scatter_about(splits[8], (INNER,), 0.5, 3.0, ((0, 4),), jnp.float32)
    conv_bc_bias = scatter_about(splits[9], (2 * STATE,), 0.5, 3.0, (), jnp.float32)
    norm_weight = jnp.clip(1.0 + 0.18 * jax.random.normal(splits[10], (INNER,), jnp.float32), 0.1, 1.9)
    return {"x_in": x_in, "bc_in": bc_in, "z_in": z_in, "dt_raw": dt_raw, "dt_bias": dt_bias, "a_log": a_log, "conv_x": conv_x, "conv_bc": conv_bc, "conv_x_bias": conv_x_bias, "conv_bc_bias": conv_bc_bias, "norm_weight": norm_weight}


def causal_conv(source, rim_rows, taps, conv_bias):
    tok_rows = source.shape[0]
    padded = jnp.concatenate([rim_rows, source], axis=0).astype(jnp.float32)
    running = conv_bias[None, :] + taps[0][None, :] * padded[0:tok_rows]
    for offset in range(1, taps.shape[0]):
        running = running + taps[offset][None, :] * padded[offset:offset + tok_rows]
    return jax.nn.silu(running).astype(jnp.bfloat16)

def span_terms(x_blk, b_blk, c_blk, step_blk, cumulative):
    length = c_blk.shape[0]
    scores = jnp.dot(c_blk, b_blk.T, preferred_element_type=jnp.float32)
    causal = jnp.arange(length)[:, None] >= jnp.arange(length)[None, :]
    log_gap = jnp.where(causal[None], cumulative[:, :, None] - cumulative[:, None, :], 0.0)
    mixing = jnp.where(causal[None], scores[None] * jnp.exp(log_gap) * step_blk[:, None, :], 0.0).astype(jnp.bfloat16)
    y_inner = jnp.einsum('htj,jhp->thp', mixing.astype(jnp.float32), x_blk.astype(jnp.float32))
    weight_in = jnp.exp(cumulative[:, -1:] - cumulative) * step_blk
    x_weighted = (x_blk.astype(jnp.float32) * weight_in.T[:, :, None]).astype(jnp.bfloat16)
    state_part = jnp.einsum('jhp,jn->hpn', x_weighted.astype(jnp.float32), b_blk.astype(jnp.float32))
    return (y_inner, state_part)

def reference(x_in, bc_in, z_in, dt_raw, dt_bias, a_log, conv_x, conv_bc, conv_x_bias, conv_bc_bias, norm_weight):
    x_conv = causal_conv(x_in, jnp.zeros((CONV - 1, x_in.shape[1]), jnp.bfloat16), conv_x, conv_x_bias)
    bc_conv = causal_conv(bc_in, jnp.zeros((CONV - 1, bc_in.shape[1]), jnp.bfloat16), conv_bc, conv_bc_bias)
    step_size = jax.nn.softplus(dt_raw + dt_bias[:, None])
    log_decay = step_size * (-jnp.exp(a_log))[:, None]
    span_count = SEQLEN // SPAN
    x_blocks = x_conv.reshape(span_count, SPAN, HEADS, HEADDIM)
    b_blocks = bc_conv[:, :STATE].reshape(span_count, SPAN, STATE)
    c_blocks = bc_conv[:, STATE:].reshape(span_count, SPAN, STATE)
    step_blocks = step_size.reshape(HEADS, span_count, SPAN).transpose(1, 0, 2)
    decay_blocks = log_decay.reshape(HEADS, span_count, SPAN).transpose(1, 0, 2)

    def advance(carried, inputs):
        x_blk, b_blk, c_blk, step_blk, decay_blk = inputs
        cumulative = jnp.cumsum(decay_blk, axis=1)
        y_inner, state_part = span_terms(x_blk, b_blk, c_blk, step_blk, cumulative)
        y_outer = jnp.einsum('tn,hpn->thp', c_blk.astype(jnp.float32), carried, precision=lax.Precision.HIGHEST)
        y_outer = y_outer * jnp.exp(cumulative).T[:, :, None]
        updated = jnp.exp(cumulative[:, -1])[:, None, None] * carried + state_part
        return (updated, y_inner + y_outer)
    final_state, y_blocks = lax.scan(advance, jnp.zeros((HEADS, HEADDIM, STATE), jnp.float32), (x_blocks, b_blocks, c_blocks, step_blocks, decay_blocks))
    y_full = y_blocks.reshape(SEQLEN, HEADS * HEADDIM)
    gated_rows = y_full * jax.nn.silu(z_in.astype(jnp.float32))
    squares = lax.optimization_barrier(jnp.sum(gated_rows * gated_rows, axis=1))
    inv_rms = lax.rsqrt(squares / (HEADS * HEADDIM) + 1e-05)
    return (gated_rows * inv_rms[:, None] * norm_weight[None, :]).astype(jnp.bfloat16)
```

```python
import functools

import jax
import jax.numpy as jnp
from jax import lax
from jax.experimental import pallas as pl
from jax.experimental.pallas import tpu as pltpu
from jax.sharding import PartitionSpec as P

HEADDIM = 64
STATE = 128
CONV = 4
LANES = 128
RIM = 8
TEAM = 4
ROWS = STATE // TEAM
COPIES = 32


f32 = jnp.float32
bf16 = jnp.bfloat16


def params(mib=24):
    return pltpu.CompilerParams(vmem_limit_bytes=mib << 20)


def cost(flops, transcendentals, nbytes):
    return pl.CostEstimate(
        flops=flops, transcendentals=transcendentals, bytes_accessed=nbytes
    )


def group(index):
    return slice(index * LANES, (index + 1) * LANES)


def half_silu(half):
    return half + half * jnp.tanh(half)


def lower_half(shape):
    return lax.broadcasted_iota(jnp.int32, shape, 1) < HEADDIM


def two_heads(by_head, index):
    shape = (by_head.shape[0], LANES)
    first = jnp.broadcast_to(by_head[:, 2 * index : 2 * index + 1], shape)
    second = jnp.broadcast_to(by_head[:, 2 * index + 1 : 2 * index + 2], shape)
    return jnp.where(lower_half(shape), first, second)


def conv_group(padded, taps, bias, tokens):
    running = bias
    for offset in range(CONV):
        first = RIM - (CONV - 1) + offset
        running = running + taps[offset : offset + 1] * padded[first : first + tokens, :]
    return half_silu(running).astype(bf16)


def conv_kernel(
    x_ref, bc_ref, rim_ref, dt_ref, head_ref, tx_ref, tb_ref, bx_ref, bb_ref,
    xc_ref, b_ref, c_ref, cum_ref, late_ref, own_ref, one_ref, two_ref, three_ref,
    padded, weighted, state, decay,
):
    tokens, width = x_ref.shape
    groups = width // LANES
    slot = lax.rem(lax.axis_index("seq"), TEAM)

    heads = dt_ref.shape[0]
    raw = jnp.concatenate(
        [dt_ref[...], jnp.zeros((COPIES - heads, tokens), f32)], axis=0
    )
    raw = jnp.concatenate([raw] * (LANES // COPIES), axis=0).T
    shifted = raw + head_ref[0:1, :]
    step = jnp.maximum(shifted, 0.0) + jnp.log1p(jnp.exp(-jnp.abs(shifted)))
    log_decay = step * -jnp.exp(head_ref[1:2, :])
    copy = lax.broadcasted_iota(jnp.int32, log_decay.shape, 1) // COPIES
    high = log_decay.astype(bf16).astype(f32)
    middle = (log_decay - high).astype(bf16).astype(f32)
    low = log_decay - high - middle
    parts = jnp.where(
        copy == 0, high, jnp.where(copy == 1, middle, jnp.where(copy == 2, low, 0.0))
    ).astype(bf16)
    causal = lax.broadcasted_iota(jnp.int32, (tokens, tokens), 0) >= (
        lax.broadcasted_iota(jnp.int32, (tokens, tokens), 1)
    )
    sums = jnp.dot(causal.astype(bf16), parts, preferred_element_type=f32)
    cum = sums
    for turn in range(1, LANES // COPIES):
        cum = cum + pltpu.roll(sums, turn * COPIES, 1)
    cum_ref[...] = cum
    late_ref[...] = (cum - jnp.log(step)).T[0:COPIES, :]
    last = cum[tokens - 1 : tokens, :]
    weight = jnp.exp(last - cum) * step
    decay[...] = jnp.broadcast_to(jnp.exp(last), (LANES, LANES)).T

    def fill(place, source, part):
        padded[place, 0:RIM, :] = rim_ref[:, part].astype(f32)
        padded[place, RIM:, :] = source.astype(f32)
        return padded.at[place]

    b_pad = fill(0, bc_ref[:, 0:STATE], slice(width, width + STATE))
    b_blk = conv_group(b_pad, 0.5 * tb_ref[:, 0:STATE], 0.5 * bb_ref[:, 0:STATE], tokens)
    b_ref[...] = b_blk
    b_turned = b_blk.astype(f32).T.astype(bf16)
    c_pad = fill(1, bc_ref[:, STATE:], slice(width + STATE, width + 2 * STATE))
    c_ref[...] = conv_group(c_pad, 0.5 * tb_ref[:, STATE:], 0.5 * bb_ref[:, STATE:], tokens)

    for index in range(groups):
        part = group(index)
        x_pad = fill(2 + index, x_ref[:, part], part)
        x_blk = conv_group(x_pad, 0.5 * tx_ref[:, part], 0.5 * bx_ref[:, part], tokens)
        xc_ref[:, part] = x_blk
        weighted[:, part] = (x_blk.astype(f32) * two_heads(weight, index)).astype(bf16)
        if index % 2 == 1 or index == groups - 1:
            first = index - index % 2
            both = slice(first * LANES, (index + 1) * LANES)
            state[:, both] = jnp.dot(
                b_turned, weighted[:, both], preferred_element_type=f32
            ).astype(bf16)

    side = jnp.concatenate(
        [
            jnp.where(
                lower_half((1, LANES)),
                decay[2 * index : 2 * index + 1, :],
                decay[2 * index + 1 : 2 * index + 2, :],
            )
            for index in range(groups)
        ]
        + [jnp.zeros((ROWS // 2 - groups, LANES), f32)],
        axis=0,
    )
    side_high = side.astype(bf16)
    side_low = (side - side_high.astype(f32)).astype(bf16)
    for turn, out_ref in enumerate((own_ref, one_ref, two_ref, three_ref)):
        rows = pl.ds(pl.multiple_of((slot ^ turn) * ROWS, ROWS), ROWS)
        out_ref[:, 0:width] = state[rows, :]
        out_ref[0 : ROWS // 2, width:] = side_high
        out_ref[ROWS // 2 :, width:] = side_low


def decays(side):
    return side[0 : ROWS // 2, :].astype(f32) + side[ROWS // 2 :, :].astype(f32)


def store_side(out_ref, width, side):
    high = side.astype(bf16)
    out_ref[0 : ROWS // 2, width:] = high
    out_ref[ROWS // 2 :, width:] = (side - high.astype(f32)).astype(bf16)


def team_kernel(own_ref, one_ref, two_ref, three_ref, whole_ref, local_ref, lead_ref, buffer):
    width = local_ref.shape[2]
    groups = width // LANES
    slot = lax.rem(lax.axis_index("seq"), TEAM)
    for turn, in_ref in enumerate((own_ref, one_ref, two_ref, three_ref)):
        buffer[slot ^ turn] = in_ref[...]
    lead = jnp.ones((ROWS // 2, LANES), f32)
    held = [jnp.zeros((ROWS, LANES), f32)] * groups
    for member in range(TEAM):
        lead_ref[member] = lead
        own = decays(buffer[member, :, width:])
        for index in range(groups):
            part = group(index)
            local_ref[member, :, part] = held[index]
            held[index] = held[index] * own[index : index + 1, :] + (
                buffer[member, :, part].astype(f32)
            )
        lead = lead * own
    for index in range(groups):
        whole_ref[:, group(index)] = held[index].astype(bf16)
    store_side(whole_ref, width, lead)


def merge_kernel(far_ref, near_ref, out_ref):
    width = out_ref.shape[1] - LANES
    near = decays(near_ref[:, width:])
    for index in range(width // LANES):
        part = group(index)
        out_ref[:, part] = (
            far_ref[:, part].astype(f32) * near[index : index + 1, :]
            + near_ref[:, part].astype(f32)
        ).astype(bf16)
    store_side(out_ref, width, near * decays(far_ref[:, width:]))


def spread_kernel(before_ref, local_ref, lead_ref, own_ref, one_ref, two_ref, three_ref):
    width = own_ref.shape[1]
    slot = lax.rem(lax.axis_index("seq"), TEAM)
    for turn, out_ref in enumerate((own_ref, one_ref, two_ref, three_ref)):
        member = slot ^ turn
        lead = lead_ref[member]
        for index in range(width // LANES):
            part = group(index)
            out_ref[:, part] = (
                before_ref[:, part].astype(f32) * lead[index : index + 1, :]
                + local_ref[member, :, part]
            ).astype(bf16)


def inner_kernel(xc_ref, b_ref, c_ref, cum_ref, late_ref, z_ref, inner_ref, outer_ref):
    tokens, width = xc_ref.shape
    half = tokens // 2
    scores = lax.dot_general(
        c_ref[...], b_ref[...], (((1,), (1,)), ((), ())), preferred_element_type=f32
    )
    causal = lax.broadcasted_iota(jnp.int32, (half, half), 0) >= (
        lax.broadcasted_iota(jnp.int32, (half, half), 1)
    )
    cum = cum_ref[...]
    grown = jnp.exp(cum)
    first = lower_half((half, LANES))
    for index in range(width // LANES):
        part = group(index)
        near, cross, far = [], [], []
        for head in (2 * index, 2 * index + 1):
            upto = jnp.broadcast_to(cum[:, head : head + 1], (tokens, half))
            early = late_ref[head : head + 1, 0:half]
            later = late_ref[head : head + 1, half:]
            near.append(
                jnp.exp(jnp.where(causal, upto[:half] - early, -1e30)) * scores[:half, :half]
            )
            cross.append(jnp.exp(upto[half:] - early) * scores[half:, :half])
            far.append(
                jnp.exp(jnp.where(causal, upto[half:] - later, -1e30)) * scores[half:, half:]
            )
        x_early = xc_ref[0:half, part]
        x_later = xc_ref[half:, part]
        zero = jnp.zeros_like(x_early)
        x_early = jnp.concatenate(
            [jnp.where(first, x_early, zero), jnp.where(first, zero, x_early)], axis=0
        )
        x_later = jnp.concatenate(
            [jnp.where(first, x_later, zero), jnp.where(first, zero, x_later)], axis=0
        )

        def times(mixing, x_blk):
            return jnp.dot(
                jnp.concatenate(mixing, axis=1).astype(bf16), x_blk, preferred_element_type=f32
            )

        y_blk = jnp.concatenate(
            [times(near, x_early), times(cross, x_early) + times(far, x_later)], axis=0
        )
        gate = half_silu(0.5 * z_ref[:, part].astype(f32))
        inner_ref[:, part] = y_blk * gate
        outer_ref[:, part] = two_heads(grown, index) * gate


def outer_kernel(
    c_ref, own_ref, one_ref, two_ref, three_ref, inner_ref, outer_ref, gated_ref, sum_ref, state
):
    tokens, width = inner_ref.shape
    slot = lax.rem(lax.axis_index("seq"), TEAM)
    for turn, in_ref in enumerate((own_ref, one_ref, two_ref, three_ref)):
        rows = pl.ds(pl.multiple_of((slot ^ turn) * ROWS, ROWS), ROWS)
        state[rows, :] = in_ref[...]
    c_blk = c_ref[...]
    total = jnp.zeros((tokens, LANES), f32)
    for index in range(width // LANES):
        part = group(index)
        y_blk = jnp.dot(c_blk, state[:, part], preferred_element_type=f32)
        gated = inner_ref[:, part] + y_blk * outer_ref[:, part]
        gated_ref[:, part] = gated
        total = total + gated * gated
    sum_ref[...] = jnp.sum(total.T, axis=0, keepdims=True)


def norm_kernel(channels, gated_ref, gain_ref, *refs):
    out_ref = refs[-1]
    whole = refs[0][...]
    for other in refs[1:-1]:
        whole = whole + other[...]
    inv_rms = lax.rsqrt(whole / channels + 1e-05)
    tokens, width = gated_ref.shape
    inv_rms = jnp.broadcast_to(inv_rms, (LANES, tokens)).T
    for index in range(width // LANES):
        part = group(index)
        out_ref[:, part] = (gated_ref[:, part] * inv_rms * gain_ref[:, part]).astype(bf16)


def call(kernel, outs, scratch=(), estimate=None, **kw):
    return pl.pallas_call(
        kernel,
        out_shape=[jax.ShapeDtypeStruct(shape, kind) for shape, kind in outs],
        scratch_shapes=[pltpu.VMEM(shape, kind) for shape, kind in scratch],
        compiler_params=params(),
        cost_estimate=estimate,
        **kw,
    )


def traded(value, axis, turn):
    peers = lax.axis_size(axis)
    return lax.ppermute(value, axis, [(i, i ^ turn) for i in range(peers)])


def moved(value, axis, by):
    peers = lax.axis_size(axis)
    return lax.ppermute(value, axis, [(i, i + by) for i in range(peers - by)])


def local(
    x_in, bc_in, z_in, dt_raw, dt_bias, a_log, conv_x, conv_bc, conv_x_bias, conv_bc_bias,
    norm_weight,
):
    tokens, width = x_in.shape
    heads = dt_raw.shape[0]
    packed = width + LANES
    teams = lax.axis_size("seq") // TEAM
    rim = moved(jnp.concatenate([x_in[-RIM:], bc_in[-RIM:]], axis=1), "seq", 1)
    by_head = jnp.pad(jnp.stack([dt_bias, a_log]), ((0, 0), (0, COPIES - heads)))
    by_head = jnp.tile(by_head, (1, LANES // COPIES))

    xc, b_blk, c_blk, cum, late, *mine = call(
        conv_kernel,
        [
            ((tokens, width), bf16),
            ((tokens, STATE), bf16),
            ((tokens, STATE), bf16),
            ((tokens, LANES), f32),
            ((COPIES, tokens), f32),
        ]
        + [((ROWS, packed), bf16)] * TEAM,
        [
            ((width // LANES + 2, RIM + tokens, LANES), f32),
            ((tokens, width), bf16),
            ((STATE, width), bf16),
            ((LANES, LANES), f32),
        ],
        cost(2 * tokens * width * STATE, tokens * width, 6 * tokens * width),
    )(
        x_in, bc_in, rim, dt_raw, by_head, conv_x, conv_bc,
        conv_x_bias[None, :], conv_bc_bias[None, :],
    )
    theirs = [mine[0]] + [traded(mine[turn], "seq", turn) for turn in range(1, TEAM)]
    inner, outer = call(
        inner_kernel,
        [((tokens, width), f32)] * 2,
        (),
        cost(6 * tokens * tokens * width // 2, tokens * tokens * heads, 14 * tokens * width),
    )(xc, b_blk, c_blk, cum, late, z_in)
    whole, team_local, lead = call(
        team_kernel,
        [
            ((ROWS, packed), bf16),
            ((TEAM, ROWS, width), f32),
            ((TEAM, ROWS // 2, LANES), f32),
        ],
        [((TEAM, ROWS, packed), bf16)],
    )(*theirs)
    before = moved(whole, "seq", TEAM)
    reach = 1
    while reach < teams - 1:
        (before,) = call(merge_kernel, [((ROWS, packed), bf16)])(
            moved(before, "seq", reach * TEAM), before
        )
        reach *= 2
    mine = call(spread_kernel, [((ROWS, width), bf16)] * TEAM)(before, team_local, lead)
    theirs = [mine[0]] + [traded(mine[turn], "seq", turn) for turn in range(1, TEAM)]
    gated, squares = call(
        outer_kernel,
        [((tokens, width), f32), ((1, tokens), f32)],
        [((STATE, width), bf16)],
    )(c_blk, *theirs, inner, outer)
    shares = lax.axis_size("head")
    sums = [squares] + [traded(squares, "head", turn) for turn in range(1, shares)]
    (y_out,) = call(
        functools.partial(norm_kernel, float(width * shares)), [((tokens, width), bf16)]
    )(gated, norm_weight[None, :], *sums)
    return y_out


def solution(mesh):
    placed = (
        P("seq", "head"),
        P("seq", None),
        P("seq", "head"),
        P("head", "seq"),
        P("head"),
        P("head"),
        P(None, "head"),
        P(),
        P("head"),
        P(),
        P("head"),
    )
    return jax.shard_map(
        local, mesh=mesh, in_specs=placed, out_specs=P("seq", "head"), check_vma=False
    )
```

```python
import functools

import jax
import jax.numpy as jnp
from jax import lax
from jax.experimental import pallas as pl
from jax.experimental.pallas import tpu as pltpu
from jax.sharding import PartitionSpec as P

HEADDIM = 64
STATE = 128
CONV = 4
LANES = 128
RIM = 8
EDGE = 16
TEAM = 4
ROWS = STATE // TEAM
COPIES = 32


f32 = jnp.float32
bf16 = jnp.bfloat16


def params(mib=24):
    return pltpu.CompilerParams(vmem_limit_bytes=mib << 20)


def cost(flops, transcendentals, nbytes):
    return pl.CostEstimate(
        flops=flops, transcendentals=transcendentals, bytes_accessed=nbytes
    )


def group(index):
    return slice(index * LANES, (index + 1) * LANES)


def half_silu(half):
    return half + half * jnp.tanh(half)


def lower_half(shape):
    return lax.broadcasted_iota(jnp.int32, shape, 1) < HEADDIM


def two_heads(by_head, index):
    shape = (by_head.shape[0], LANES)
    first = jnp.broadcast_to(by_head[:, 2 * index : 2 * index + 1], shape)
    second = jnp.broadcast_to(by_head[:, 2 * index + 1 : 2 * index + 2], shape)
    return jnp.where(lower_half(shape), first, second)


def conv_group(padded, taps, bias, tokens):
    running = bias
    for offset in range(CONV):
        first = RIM - (CONV - 1) + offset
        running = running + taps[offset : offset + 1] * padded[first : first + tokens, :]
    return half_silu(running).astype(bf16)


def fetch(sources, targets, semaphores):
    copies = [
        pltpu.make_async_copy(source, target, semaphores.at[place])
        for place, (source, target) in enumerate(zip(sources, targets))
    ]
    for copy in copies:
        copy.start()
    return copies


def rim_kernel(x_ref, bc_ref, rim_ref, semaphores):
    tokens, width = x_ref.shape
    last = slice(tokens - RIM, tokens)
    copies = fetch(
        (x_ref.at[last, :], bc_ref.at[last, :]),
        (rim_ref.at[:, 0:width], rim_ref.at[:, width:]),
        semaphores,
    )
    for copy in copies:
        copy.wait()


def scan_decay(raw, bias, rate):
    tokens = raw.shape[1]
    blank = jnp.zeros((LANES - raw.shape[0], tokens), f32)
    shifted = jnp.concatenate([raw, blank], axis=0).T + bias
    step = jnp.maximum(shifted, 0.0) + jnp.log1p(jnp.exp(-jnp.abs(shifted)))
    log_decay = step * -jnp.exp(rate)
    causal = lax.broadcasted_iota(jnp.int32, (tokens, tokens), 0) >= (
        lax.broadcasted_iota(jnp.int32, (tokens, tokens), 1)
    )
    causal = causal.astype(bf16)
    cum = 0.0
    for _ in range(3):
        part = log_decay.astype(bf16)
        log_decay = log_decay - part.astype(f32)
        cum = cum + jnp.dot(causal, part, preferred_element_type=f32)
    return step, cum


def early_kernel(
    x_hbm, bc_hbm, dt_hbm, bias_hbm, rate_hbm, tx_hbm, tb_hbm, bx_hbm, bb_hbm,
    xc_ref, b_ref, c_ref, cum_ref, late_ref, state_ref, weight_ref, side_ref, edge_ref,
    tx_ref, tb_ref, bx_ref, bb_ref,
    x_ref, bc_ref, dt_ref, bias_ref, rate_ref, padded, weighted, decay, semaphores,
):
    tokens, width = x_ref.shape
    groups = width // LANES
    chunks = width // (2 * LANES)
    small = fetch(
        (dt_hbm, bias_hbm, rate_hbm, bc_hbm, tb_hbm, bb_hbm, tx_hbm, bx_hbm),
        (dt_ref, bias_ref, rate_ref, bc_ref, tb_ref, bb_ref, tx_ref, bx_ref),
        semaphores,
    )
    large = fetch(
        [x_hbm.at[:, pl.ds(2 * LANES * place, 2 * LANES)] for place in range(chunks)],
        [x_ref.at[:, pl.ds(2 * LANES * place, 2 * LANES)] for place in range(chunks)],
        semaphores.at[pl.ds(len(small), chunks)],
    )
    for copy in small[0:3]:
        copy.wait()
    heads = dt_ref.shape[0]
    blank = jnp.zeros((1, LANES - heads), f32)
    step, cum = scan_decay(
        dt_ref[...],
        jnp.concatenate([bias_ref[...], blank], axis=1),
        jnp.concatenate([rate_ref[...], blank], axis=1),
    )
    cum_ref[...] = cum
    late_ref[...] = (cum - jnp.log(step)).T[0:COPIES, :]
    last = cum[tokens - 1 : tokens, :]
    weight = jnp.exp(last - cum) * step
    weight_ref[...] = weight[0:EDGE, :]
    inside = lax.broadcasted_iota(jnp.int32, weight.shape, 0) >= EDGE
    weight = jnp.where(inside, weight, 0.0)
    decay[...] = jnp.broadcast_to(jnp.exp(last), (LANES, LANES)).T
    side = jnp.concatenate(
        [
            jnp.where(
                lower_half((1, LANES)),
                decay[2 * index : 2 * index + 1, :],
                decay[2 * index + 1 : 2 * index + 2, :],
            )
            for index in range(groups)
        ]
        + [jnp.zeros((ROWS // 2 - groups, LANES), f32)],
        axis=0,
    )
    store_side(side_ref, 0, side)

    def fill(place, source):
        padded[place, 0:RIM, :] = jnp.zeros((RIM, LANES), f32)
        padded[place, RIM:, :] = source.astype(f32)
        return padded.at[place]

    for copy in small[3:6]:
        copy.wait()
    b_pad = fill(0, bc_ref[:, 0:STATE])
    b_blk = conv_group(b_pad, 0.5 * tb_ref[:, 0:STATE], 0.5 * bb_ref[0:1, :], tokens)
    b_ref[...] = b_blk
    b_turned = b_blk.astype(f32).T.astype(bf16)
    c_pad = fill(1, bc_ref[:, STATE:])
    c_ref[...] = conv_group(c_pad, 0.5 * tb_ref[:, STATE:], 0.5 * bb_ref[1:2, :], tokens)
    edge_ref[:, width:] = bc_ref[0:EDGE, :]
    for copy in small[6:8]:
        copy.wait()
    for index in range(groups):
        part = group(index)
        if index % 2 == 0:
            large[index // 2].wait()
        x_pad = fill(2 + index, x_ref[:, part])
        x_blk = conv_group(
            x_pad, 0.5 * tx_ref[:, part], 0.5 * bx_ref[index : index + 1, :], tokens
        )
        xc_ref[:, part] = x_blk
        edge_ref[:, part] = x_ref[0:EDGE, part]
        weighted[:, part] = (x_blk.astype(f32) * two_heads(weight, index)).astype(bf16)
        if index % 2 == 1:
            both = slice((index - 1) * LANES, (index + 1) * LANES)
            state_ref[:, both] = jnp.dot(
                b_turned, weighted[:, both], preferred_element_type=f32
            )


def edge_kernel(
    rim_ref, edge_ref, tx_ref, tb_ref, bx_ref, bb_ref, weight_ref, state_ref, side_ref,
    x_ref, b_ref, c_ref, own_ref, one_ref, two_ref, three_ref,
    padded, weighted, state,
):
    width = x_ref.shape[1]
    slot = lax.rem(lax.axis_index("seq"), TEAM)

    def fill(place, part):
        padded[place, 0:RIM, :] = rim_ref[:, part].astype(f32)
        padded[place, RIM:, :] = edge_ref[:, part].astype(f32)
        return padded.at[place]

    b_pad = fill(0, slice(width, width + STATE))
    b_blk = conv_group(b_pad, 0.5 * tb_ref[:, 0:STATE], 0.5 * bb_ref[0:1, :], EDGE)
    b_ref[...] = b_blk
    b_turned = b_blk.astype(f32).T.astype(bf16)
    c_pad = fill(1, slice(width + STATE, width + 2 * STATE))
    c_ref[...] = conv_group(c_pad, 0.5 * tb_ref[:, STATE:], 0.5 * bb_ref[1:2, :], EDGE)
    weight = weight_ref[...]
    for index in range(width // LANES):
        part = group(index)
        x_pad = fill(2 + index, part)
        x_blk = conv_group(
            x_pad, 0.5 * tx_ref[:, part], 0.5 * bx_ref[index : index + 1, :], EDGE
        )
        x_ref[:, part] = x_blk
        weighted[:, part] = (x_blk.astype(f32) * two_heads(weight, index)).astype(bf16)
        if index % 2 == 1:
            both = slice((index - 1) * LANES, (index + 1) * LANES)
            state[:, both] = (
                state_ref[:, both]
                + jnp.dot(b_turned, weighted[:, both], preferred_element_type=f32)
            ).astype(bf16)
    for turn, out_ref in enumerate((own_ref, one_ref, two_ref, three_ref)):
        rows = pl.ds(pl.multiple_of((slot ^ turn) * ROWS, ROWS), ROWS)
        out_ref[:, 0:width] = state[rows, :]
        out_ref[:, width:] = side_ref[...]


def decays(side):
    return side[0 : ROWS // 2, :].astype(f32) + side[ROWS // 2 :, :].astype(f32)


def store_side(out_ref, width, side):
    high = side.astype(bf16)
    out_ref[0 : ROWS // 2, width:] = high
    out_ref[ROWS // 2 :, width:] = (side - high.astype(f32)).astype(bf16)


def team_kernel(own_ref, one_ref, two_ref, three_ref, whole_ref, local_ref, lead_ref, buffer):
    width = local_ref.shape[2]
    groups = width // LANES
    slot = lax.rem(lax.axis_index("seq"), TEAM)
    for turn, in_ref in enumerate((own_ref, one_ref, two_ref, three_ref)):
        buffer[slot ^ turn] = in_ref[...]
    lead = jnp.ones((ROWS // 2, LANES), f32)
    held = [jnp.zeros((ROWS, LANES), f32)] * groups
    for member in range(TEAM):
        lead_ref[member] = lead
        own = decays(buffer[member, :, width:])
        for index in range(groups):
            part = group(index)
            local_ref[member, :, part] = held[index]
            held[index] = held[index] * own[index : index + 1, :] + (
                buffer[member, :, part].astype(f32)
            )
        lead = lead * own
    for index in range(groups):
        whole_ref[:, group(index)] = held[index].astype(bf16)
    store_side(whole_ref, width, lead)


def merge_kernel(far_ref, near_ref, out_ref):
    width = out_ref.shape[1] - LANES
    near = decays(near_ref[:, width:])
    for index in range(width // LANES):
        part = group(index)
        out_ref[:, part] = (
            far_ref[:, part].astype(f32) * near[index : index + 1, :]
            + near_ref[:, part].astype(f32)
        ).astype(bf16)
    store_side(out_ref, width, near * decays(far_ref[:, width:]))


def spread_kernel(before_ref, local_ref, lead_ref, own_ref, one_ref, two_ref, three_ref):
    width = own_ref.shape[1]
    place = lax.axis_index("seq")
    slot = lax.rem(place, TEAM)
    for turn, out_ref in enumerate((own_ref, one_ref, two_ref, three_ref)):
        member = slot ^ turn
        lead = jnp.where(place >= TEAM, lead_ref[member], 0.0)
        for index in range(width // LANES):
            part = group(index)
            out_ref[:, part] = (
                before_ref[:, part].astype(f32) * lead[index : index + 1, :]
                + local_ref[member, :, part]
            ).astype(bf16)


def inner_kernel(
    xc_ref, b_part, c_part, x_edge, b_edge, c_edge, cum_ref, late_ref, z_ref,
    inner_ref, outer_ref, c_ref,
):
    tokens, width = xc_ref.shape
    half = tokens // 2
    b_blk = jnp.concatenate([b_edge[...], b_part[EDGE:, :]], axis=0)
    c_blk = jnp.concatenate([c_edge[...], c_part[EDGE:, :]], axis=0)
    c_ref[...] = c_blk
    scores = lax.dot_general(
        c_blk, b_blk, (((1,), (1,)), ((), ())), preferred_element_type=f32
    )
    causal = lax.broadcasted_iota(jnp.int32, (half, half), 0) >= (
        lax.broadcasted_iota(jnp.int32, (half, half), 1)
    )
    cum = cum_ref[...]
    grown = jnp.exp(cum)
    first = lower_half((half, LANES))
    for index in range(width // LANES):
        part = group(index)
        near, cross, far = [], [], []
        for head in (2 * index, 2 * index + 1):
            upto = jnp.broadcast_to(cum[:, head : head + 1], (tokens, half))
            early = late_ref[head : head + 1, 0:half]
            later = late_ref[head : head + 1, half:]
            near.append(
                jnp.exp(jnp.where(causal, upto[:half] - early, -1e30)) * scores[:half, :half]
            )
            cross.append(jnp.exp(upto[half:] - early) * scores[half:, :half])
            far.append(
                jnp.exp(jnp.where(causal, upto[half:] - later, -1e30)) * scores[half:, half:]
            )
        x_early = jnp.concatenate([x_edge[:, part], xc_ref[EDGE:half, part]], axis=0)
        x_later = xc_ref[half:, part]
        zero = jnp.zeros_like(x_early)
        x_early = jnp.concatenate(
            [jnp.where(first, x_early, zero), jnp.where(first, zero, x_early)], axis=0
        )
        x_later = jnp.concatenate(
            [jnp.where(first, x_later, zero), jnp.where(first, zero, x_later)], axis=0
        )

        def times(mixing, x_blk):
            return jnp.dot(
                jnp.concatenate(mixing, axis=1).astype(bf16), x_blk, preferred_element_type=f32
            )

        y_blk = jnp.concatenate(
            [times(near, x_early), times(cross, x_early) + times(far, x_later)], axis=0
        )
        gate = half_silu(0.5 * z_ref[:, part].astype(f32))
        inner_ref[:, part] = y_blk * gate
        outer_ref[:, part] = two_heads(grown, index) * gate


def outer_kernel(
    c_ref, own_ref, one_ref, two_ref, three_ref, inner_ref, outer_ref, gated_ref, sum_ref, state
):
    tokens, width = inner_ref.shape
    slot = lax.rem(lax.axis_index("seq"), TEAM)
    for turn, in_ref in enumerate((own_ref, one_ref, two_ref, three_ref)):
        rows = pl.ds(pl.multiple_of((slot ^ turn) * ROWS, ROWS), ROWS)
        state[rows, :] = in_ref[...]
    c_blk = c_ref[...]
    total = jnp.zeros((tokens, LANES), f32)
    for index in range(width // LANES):
        part = group(index)
        y_blk = jnp.dot(c_blk, state[:, part], preferred_element_type=f32)
        gated = inner_ref[:, part] + y_blk * outer_ref[:, part]
        gated_ref[:, part] = gated
        total = total + gated * gated
    sum_ref[...] = jnp.sum(total.T, axis=0, keepdims=True)


def norm_kernel(channels, gated_ref, gain_ref, *refs):
    out_hbm, out_ref, semaphores = refs[-3:]
    whole = refs[0][...]
    for other in refs[1:-3]:
        whole = whole + other[...]
    inv_rms = lax.rsqrt(whole / channels + 1e-05)
    tokens, width = gated_ref.shape
    inv_rms = jnp.broadcast_to(inv_rms, (LANES, tokens)).T
    pieces = semaphores.shape[0]
    rows = tokens // pieces
    copies = []
    for piece in range(pieces):
        block = slice(piece * rows, (piece + 1) * rows)
        for index in range(width // LANES):
            part = group(index)
            out_ref[block, part] = (
                gated_ref[block, part] * inv_rms[block, :] * gain_ref[index : index + 1, :]
            ).astype(bf16)
        copy = pltpu.make_async_copy(
            out_ref.at[block, :], out_hbm.at[block, :], semaphores.at[piece]
        )
        copy.start()
        copies.append(copy)
    for copy in copies:
        copy.wait()


def call(kernel, outs, scratch=(), copies=0, estimate=None, **kw):
    return pl.pallas_call(
        kernel,
        out_shape=[jax.ShapeDtypeStruct(shape, kind) for shape, kind in outs],
        scratch_shapes=[pltpu.VMEM(shape, kind) for shape, kind in scratch]
        + [pltpu.SemaphoreType.DMA((copies,))] * (copies > 0),
        compiler_params=params(),
        cost_estimate=estimate,
        **kw,
    )


def traded(value, axis, turn):
    peers = lax.axis_size(axis)
    return lax.ppermute(value, axis, [(i, i ^ turn) for i in range(peers)])


def moved(value, axis, by):
    peers = lax.axis_size(axis)
    return lax.ppermute(value, axis, [(i, i + by) for i in range(peers - by)])


def local(
    x_in, bc_in, z_in, dt_raw, dt_bias, a_log, conv_x, conv_bc, conv_x_bias, conv_bc_bias,
    norm_weight,
):
    tokens, width = x_in.shape
    heads = dt_raw.shape[0]
    packed = width + LANES
    groups = width // LANES
    teams = lax.axis_size("seq") // TEAM
    hbm = pl.BlockSpec(memory_space=pltpu.MemorySpace.HBM)
    (rim,) = call(
        rim_kernel, [((RIM, width + 2 * STATE), bf16)], (), 2, in_specs=[hbm] * 2
    )(x_in, bc_in)
    rim = moved(rim, "seq", 1)
    xc, b_blk, c_blk, cum, late, state, weight, side, edge, *taps = call(
        early_kernel,
        [
            ((tokens, width), bf16),
            ((tokens, STATE), bf16),
            ((tokens, STATE), bf16),
            ((tokens, LANES), f32),
            ((COPIES, tokens), f32),
            ((STATE, width), f32),
            ((EDGE, LANES), f32),
            ((ROWS, LANES), bf16),
            ((EDGE, width + 2 * STATE), bf16),
            ((CONV, width), f32),
            ((CONV, 2 * STATE), f32),
            ((groups, LANES), f32),
            ((2, STATE), f32),
        ],
        [
            ((tokens, width), bf16),
            ((tokens, 2 * STATE), bf16),
            ((heads, tokens), f32),
            ((1, heads), f32),
            ((1, heads), f32),
            ((groups + 2, RIM + tokens, LANES), f32),
            ((tokens, width), bf16),
            ((LANES, LANES), f32),
        ],
        8 + groups // 2,
        cost(2 * tokens * width * STATE, tokens * width, 6 * tokens * width),
        in_specs=[hbm] * 9,
    )(
        x_in, bc_in, dt_raw, dt_bias[None, :], a_log[None, :], conv_x, conv_bc,
        conv_x_bias.reshape(groups, LANES), conv_bc_bias.reshape(2, STATE),
    )
    x_edge, b_edge, c_edge, *mine = call(
        edge_kernel,
        [((EDGE, width), bf16), ((EDGE, STATE), bf16), ((EDGE, STATE), bf16)]
        + [((ROWS, packed), bf16)] * TEAM,
        [
            ((groups + 2, RIM + EDGE, LANES), f32),
            ((EDGE, width), bf16),
            ((STATE, width), bf16),
        ],
    )(rim, edge, *taps, weight, state, side)
    theirs = [mine[0]] + [traded(mine[turn], "seq", turn) for turn in range(1, TEAM)]
    inner, outer, c_blk = call(
        inner_kernel,
        [((tokens, width), f32)] * 2 + [((tokens, STATE), bf16)],
        (),
        0,
        cost(6 * tokens * tokens * width // 2, tokens * tokens * heads, 14 * tokens * width),
    )(xc, b_blk, c_blk, x_edge, b_edge, c_edge, cum, late, z_in)
    whole, team_local, lead = call(
        team_kernel,
        [
            ((ROWS, packed), bf16),
            ((TEAM, ROWS, width), f32),
            ((TEAM, ROWS // 2, LANES), f32),
        ],
        [((TEAM, ROWS, packed), bf16)],
    )(*theirs)
    before = traded(whole, "seq", TEAM) if teams == 2 else moved(whole, "seq", TEAM)
    reach = 1
    while reach < teams - 1:
        (before,) = call(merge_kernel, [((ROWS, packed), bf16)])(
            moved(before, "seq", reach * TEAM), before
        )
        reach *= 2
    before, inner, outer, c_blk = lax.optimization_barrier((before, inner, outer, c_blk))
    mine = call(spread_kernel, [((ROWS, width), bf16)] * TEAM)(before, team_local, lead)
    theirs = [mine[0]] + [traded(mine[turn], "seq", turn) for turn in range(1, TEAM)]
    gated, squares = call(
        outer_kernel,
        [((tokens, width), f32), ((1, tokens), f32)],
        [((STATE, width), bf16)],
    )(c_blk, *theirs, inner, outer)
    shares = lax.axis_size("head")
    sums = [squares] + [traded(squares, "head", turn) for turn in range(1, shares)]
    (y_out,) = call(
        functools.partial(norm_kernel, float(width * shares)),
        [((tokens, width), bf16)],
        [((tokens, width), bf16)],
        4,
        out_specs=[hbm],
    )(gated, norm_weight.reshape(groups, LANES), *sums)
    return y_out


def solution(mesh):
    placed = (
        P("seq", "head"),
        P("seq", None),
        P("seq", "head"),
        P("head", "seq"),
        P("head"),
        P("head"),
        P(None, "head"),
        P(),
        P("head"),
        P(),
        P("head"),
    )
    return jax.shard_map(
        local, mesh=mesh, in_specs=placed, out_specs=P("seq", "head"), check_vma=False
    )
```

```python
import functools

import jax
import jax.numpy as jnp
from jax import lax
from jax.experimental import pallas as pl
from jax.experimental.pallas import tpu as pltpu
from jax.sharding import PartitionSpec as P

HEADDIM = 64
STATE = 128
CONV = 4
LANES = 128
RIM = 8
EDGE = 16
TEAM = 4
ROWS = STATE // TEAM
COPIES = 32


f32 = jnp.float32
bf16 = jnp.bfloat16


def params(mib=24):
    return pltpu.CompilerParams(vmem_limit_bytes=mib << 20)


def cost(flops, transcendentals, nbytes):
    return pl.CostEstimate(
        flops=flops, transcendentals=transcendentals, bytes_accessed=nbytes
    )


def group(index):
    return slice(index * LANES, (index + 1) * LANES)


def half_silu(half):
    return half + half * jnp.tanh(half)


def lower_half(shape):
    return lax.broadcasted_iota(jnp.int32, shape, 1) < HEADDIM


def two_heads(by_head, index):
    shape = (by_head.shape[0], LANES)
    first = jnp.broadcast_to(by_head[:, 2 * index : 2 * index + 1], shape)
    second = jnp.broadcast_to(by_head[:, 2 * index + 1 : 2 * index + 2], shape)
    return jnp.where(lower_half(shape), first, second)


def conv_group(padded, taps, bias, tokens):
    running = bias
    for offset in range(CONV):
        first = RIM - (CONV - 1) + offset
        running = running + taps[offset : offset + 1] * padded[first : first + tokens, :]
    return half_silu(running).astype(bf16)


def fetch(sources, targets, semaphores):
    copies = [
        pltpu.make_async_copy(source, target, semaphores.at[place])
        for place, (source, target) in enumerate(zip(sources, targets))
    ]
    for copy in copies:
        copy.start()
    return copies


def rim_kernel(x_ref, bc_ref, rim_ref, semaphores):
    tokens, width = x_ref.shape
    last = slice(tokens - RIM, tokens)
    copies = fetch(
        (x_ref.at[last, :], bc_ref.at[last, :]),
        (rim_ref.at[:, 0:width], rim_ref.at[:, width:]),
        semaphores,
    )
    for copy in copies:
        copy.wait()


def scan_decay(raw, bias, rate):
    tokens = raw.shape[1]
    blank = jnp.zeros((LANES - raw.shape[0], tokens), f32)
    shifted = jnp.concatenate([raw, blank], axis=0).T + bias
    step = jnp.maximum(shifted, 0.0) + jnp.log1p(jnp.exp(-jnp.abs(shifted)))
    log_decay = step * -jnp.exp(rate)
    causal = lax.broadcasted_iota(jnp.int32, (tokens, tokens), 0) >= (
        lax.broadcasted_iota(jnp.int32, (tokens, tokens), 1)
    )
    causal = causal.astype(bf16)
    cum = 0.0
    for _ in range(3):
        part = log_decay.astype(bf16)
        log_decay = log_decay - part.astype(f32)
        cum = cum + jnp.dot(causal, part, preferred_element_type=f32)
    return step, cum


def early_kernel(
    x_hbm, bc_hbm, dt_hbm, bias_hbm, rate_hbm, tx_hbm, tb_hbm, bx_hbm, bb_hbm,
    xc_ref, b_ref, c_ref, cum_ref, late_ref, state_ref, weight_ref, side_ref, edge_ref,
    tx_ref, tb_ref, bx_ref, bb_ref,
    x_ref, bc_ref, dt_ref, bias_ref, rate_ref, padded, weighted, decay, semaphores,
):
    tokens, width = x_ref.shape
    groups = width // LANES
    chunks = width // (2 * LANES)
    small = fetch(
        (dt_hbm, bias_hbm, rate_hbm, bc_hbm, tb_hbm, bb_hbm, tx_hbm, bx_hbm),
        (dt_ref, bias_ref, rate_ref, bc_ref, tb_ref, bb_ref, tx_ref, bx_ref),
        semaphores,
    )
    large = fetch(
        [x_hbm.at[:, pl.ds(2 * LANES * place, 2 * LANES)] for place in range(chunks)],
        [x_ref.at[:, pl.ds(2 * LANES * place, 2 * LANES)] for place in range(chunks)],
        semaphores.at[pl.ds(len(small), chunks)],
    )
    for copy in small[0:3]:
        copy.wait()
    heads = dt_ref.shape[0]
    blank = jnp.zeros((1, LANES - heads), f32)
    step, cum = scan_decay(
        dt_ref[...],
        jnp.concatenate([bias_ref[...], blank], axis=1),
        jnp.concatenate([rate_ref[...], blank], axis=1),
    )
    cum_ref[...] = cum
    late_ref[...] = (cum - jnp.log(step)).T[0:COPIES, :]
    last = cum[tokens - 1 : tokens, :]
    weight = jnp.exp(last - cum) * step
    weight_ref[...] = weight[0:EDGE, :]
    inside = lax.broadcasted_iota(jnp.int32, weight.shape, 0) >= EDGE
    weight = jnp.where(inside, weight, 0.0)
    decay[...] = jnp.broadcast_to(jnp.exp(last), (LANES, LANES)).T
    side = jnp.concatenate(
        [
            jnp.where(
                lower_half((1, LANES)),
                decay[2 * index : 2 * index + 1, :],
                decay[2 * index + 1 : 2 * index + 2, :],
            )
            for index in range(groups)
        ]
        + [jnp.zeros((ROWS // 2 - groups, LANES), f32)],
        axis=0,
    )
    store_side(side_ref, 0, side)

    def fill(place, source):
        padded[place, 0:RIM, :] = jnp.zeros((RIM, LANES), f32)
        padded[place, RIM:, :] = source.astype(f32)
        return padded.at[place]

    for copy in small[3:6]:
        copy.wait()
    b_pad = fill(0, bc_ref[:, 0:STATE])
    b_blk = conv_group(b_pad, 0.5 * tb_ref[:, 0:STATE], 0.5 * bb_ref[0:1, :], tokens)
    b_ref[...] = b_blk
    b_turned = b_blk.astype(f32).T.astype(bf16)
    c_pad = fill(1, bc_ref[:, STATE:])
    c_ref[...] = conv_group(c_pad, 0.5 * tb_ref[:, STATE:], 0.5 * bb_ref[1:2, :], tokens)
    edge_ref[:, width:] = bc_ref[0:EDGE, :]
    for copy in small[6:8]:
        copy.wait()
    for index in range(groups):
        part = group(index)
        if index % 2 == 0:
            large[index // 2].wait()
        x_pad = fill(2 + index, x_ref[:, part])
        x_blk = conv_group(
            x_pad, 0.5 * tx_ref[:, part], 0.5 * bx_ref[index : index + 1, :], tokens
        )
        xc_ref[:, part] = x_blk
        edge_ref[:, part] = x_ref[0:EDGE, part]
        weighted[:, part] = (x_blk.astype(f32) * two_heads(weight, index)).astype(bf16)
        if index % 2 == 1:
            both = slice((index - 1) * LANES, (index + 1) * LANES)
            state_ref[:, both] = jnp.dot(
                b_turned, weighted[:, both], preferred_element_type=f32
            )


def edge_kernel(
    rim_ref, edge_ref, tx_ref, tb_ref, bx_ref, bb_ref, weight_ref, state_ref, side_ref,
    x_ref, b_ref, c_ref, own_ref, one_ref, two_ref, three_ref,
    padded, weighted, state,
):
    width = x_ref.shape[1]
    slot = lax.rem(lax.axis_index("seq"), TEAM)

    def fill(place, part):
        padded[place, 0:RIM, :] = rim_ref[:, part].astype(f32)
        padded[place, RIM:, :] = edge_ref[:, part].astype(f32)
        return padded.at[place]

    b_pad = fill(0, slice(width, width + STATE))
    b_blk = conv_group(b_pad, 0.5 * tb_ref[:, 0:STATE], 0.5 * bb_ref[0:1, :], EDGE)
    b_ref[...] = b_blk
    b_turned = b_blk.astype(f32).T.astype(bf16)
    c_pad = fill(1, slice(width + STATE, width + 2 * STATE))
    c_ref[...] = conv_group(c_pad, 0.5 * tb_ref[:, STATE:], 0.5 * bb_ref[1:2, :], EDGE)
    weight = weight_ref[...]
    for index in range(width // LANES):
        part = group(index)
        x_pad = fill(2 + index, part)
        x_blk = conv_group(
            x_pad, 0.5 * tx_ref[:, part], 0.5 * bx_ref[index : index + 1, :], EDGE
        )
        x_ref[:, part] = x_blk
        weighted[:, part] = (x_blk.astype(f32) * two_heads(weight, index)).astype(bf16)
        if index % 2 == 1:
            both = slice((index - 1) * LANES, (index + 1) * LANES)
            state[:, both] = (
                state_ref[:, both]
                + jnp.dot(b_turned, weighted[:, both], preferred_element_type=f32)
            ).astype(bf16)
    for turn, out_ref in enumerate((own_ref, one_ref, two_ref, three_ref)):
        rows = pl.ds(pl.multiple_of((slot ^ turn) * ROWS, ROWS), ROWS)
        out_ref[:, 0:width] = state[rows, :]
        out_ref[:, width:] = side_ref[...]


def decays(side):
    return side[0 : ROWS // 2, :].astype(f32) + side[ROWS // 2 :, :].astype(f32)


def store_side(out_ref, width, side):
    high = side.astype(bf16)
    out_ref[0 : ROWS // 2, width:] = high
    out_ref[ROWS // 2 :, width:] = (side - high.astype(f32)).astype(bf16)


def team_kernel(own_ref, one_ref, two_ref, three_ref, whole_ref, local_ref, lead_ref, buffer):
    width = local_ref.shape[2]
    groups = width // LANES
    slot = lax.rem(lax.axis_index("seq"), TEAM)
    for turn, in_ref in enumerate((own_ref, one_ref, two_ref, three_ref)):
        buffer[slot ^ turn] = in_ref[...]
    lead = jnp.ones((ROWS // 2, LANES), f32)
    held = [jnp.zeros((ROWS, LANES), f32)] * groups
    for member in range(TEAM):
        lead_ref[member] = lead
        own = decays(buffer[member, :, width:])
        for index in range(groups):
            part = group(index)
            local_ref[member, :, part] = held[index]
            held[index] = held[index] * own[index : index + 1, :] + (
                buffer[member, :, part].astype(f32)
            )
        lead = lead * own
    for index in range(groups):
        whole_ref[:, group(index)] = held[index].astype(bf16)
    store_side(whole_ref, width, lead)


def merge_kernel(far_ref, near_ref, out_ref):
    width = out_ref.shape[1] - LANES
    near = decays(near_ref[:, width:])
    for index in range(width // LANES):
        part = group(index)
        out_ref[:, part] = (
            far_ref[:, part].astype(f32) * near[index : index + 1, :]
            + near_ref[:, part].astype(f32)
        ).astype(bf16)
    store_side(out_ref, width, near * decays(far_ref[:, width:]))


def spread_kernel(before_ref, local_ref, lead_ref, own_ref, one_ref, two_ref, three_ref):
    width = own_ref.shape[1]
    place = lax.axis_index("seq")
    slot = lax.rem(place, TEAM)
    for turn, out_ref in enumerate((own_ref, one_ref, two_ref, three_ref)):
        member = slot ^ turn
        lead = jnp.where(place >= TEAM, lead_ref[member], 0.0)
        for index in range(width // LANES):
            part = group(index)
            out_ref[:, part] = (
                before_ref[:, part].astype(f32) * lead[index : index + 1, :]
                + local_ref[member, :, part]
            ).astype(bf16)


def inner_kernel(
    xc_ref, b_part, c_part, x_edge, b_edge, c_edge, cum_ref, late_ref, z_ref,
    inner_ref, outer_ref, c_ref,
):
    tokens, width = xc_ref.shape
    half = tokens // 2
    b_blk = jnp.concatenate([b_edge[...], b_part[EDGE:, :]], axis=0)
    c_blk = jnp.concatenate([c_edge[...], c_part[EDGE:, :]], axis=0)
    c_ref[...] = c_blk
    scores = lax.dot_general(
        c_blk, b_blk, (((1,), (1,)), ((), ())), preferred_element_type=f32
    )
    causal = lax.broadcasted_iota(jnp.int32, (half, half), 0) >= (
        lax.broadcasted_iota(jnp.int32, (half, half), 1)
    )
    cum = cum_ref[...]
    grown = jnp.exp(cum)
    first = lower_half((half, LANES))
    for index in range(width // LANES):
        part = group(index)
        near, cross, far = [], [], []
        for head in (2 * index, 2 * index + 1):
            upto = jnp.broadcast_to(cum[:, head : head + 1], (tokens, half))
            early = late_ref[head : head + 1, 0:half]
            later = late_ref[head : head + 1, half:]
            near.append(
                jnp.exp(jnp.where(causal, upto[:half] - early, -1e30)) * scores[:half, :half]
            )
            cross.append(jnp.exp(upto[half:] - early) * scores[half:, :half])
            far.append(
                jnp.exp(jnp.where(causal, upto[half:] - later, -1e30)) * scores[half:, half:]
            )
        x_early = jnp.concatenate([x_edge[:, part], xc_ref[EDGE:half, part]], axis=0)
        x_later = xc_ref[half:, part]
        zero = jnp.zeros_like(x_early)
        x_early = jnp.concatenate(
            [jnp.where(first, x_early, zero), jnp.where(first, zero, x_early)], axis=0
        )
        x_later = jnp.concatenate(
            [jnp.where(first, x_later, zero), jnp.where(first, zero, x_later)], axis=0
        )

        def times(mixing, x_blk):
            return jnp.dot(
                jnp.concatenate(mixing, axis=1).astype(bf16), x_blk, preferred_element_type=f32
            )

        y_blk = jnp.concatenate(
            [times(near, x_early), times(cross, x_early) + times(far, x_later)], axis=0
        )
        gate = half_silu(0.5 * z_ref[:, part].astype(f32))
        inner_ref[:, part] = y_blk * gate
        outer_ref[:, part] = two_heads(grown, index) * gate


def outer_kernel(
    c_ref, own_ref, one_ref, two_ref, three_ref, inner_ref, outer_ref, gated_ref, sum_ref, state
):
    tokens, width = inner_ref.shape
    slot = lax.rem(lax.axis_index("seq"), TEAM)
    for turn, in_ref in enumerate((own_ref, one_ref, two_ref, three_ref)):
        rows = pl.ds(pl.multiple_of((slot ^ turn) * ROWS, ROWS), ROWS)
        state[rows, :] = in_ref[...]
    c_blk = c_ref[...]
    total = jnp.zeros((tokens, LANES), f32)
    for index in range(width // LANES):
        part = group(index)
        y_blk = jnp.dot(c_blk, state[:, part], preferred_element_type=f32)
        gated = inner_ref[:, part] + y_blk * outer_ref[:, part]
        gated_ref[:, part] = gated
        total = total + gated * gated
    sum_ref[...] = jnp.sum(total.T, axis=0, keepdims=True)


def norm_kernel(channels, gated_ref, gain_ref, *refs):
    out_hbm, out_ref, semaphores = refs[-3:]
    whole = refs[0][...]
    for other in refs[1:-3]:
        whole = whole + other[...]
    inv_rms = lax.rsqrt(whole / channels + 1e-05)
    tokens, width = gated_ref.shape
    inv_rms = jnp.broadcast_to(inv_rms, (LANES, tokens)).T
    pieces = semaphores.shape[0]
    rows = tokens // pieces
    copies = []
    for piece in range(pieces):
        block = slice(piece * rows, (piece + 1) * rows)
        for index in range(width // LANES):
            part = group(index)
            out_ref[block, part] = (
                gated_ref[block, part] * inv_rms[block, :] * gain_ref[index : index + 1, :]
            ).astype(bf16)
        copy = pltpu.make_async_copy(
            out_ref.at[block, :], out_hbm.at[block, :], semaphores.at[piece]
        )
        copy.start()
        copies.append(copy)
    for copy in copies:
        copy.wait()


def call(kernel, outs, scratch=(), copies=0, estimate=None, **kw):
    return pl.pallas_call(
        kernel,
        out_shape=[jax.ShapeDtypeStruct(shape, kind) for shape, kind in outs],
        scratch_shapes=[pltpu.VMEM(shape, kind) for shape, kind in scratch]
        + [pltpu.SemaphoreType.DMA((copies,))] * (copies > 0),
        compiler_params=params(),
        cost_estimate=estimate,
        **kw,
    )


def pinned(value):
    return pltpu.with_memory_space_constraint(value, pltpu.MemorySpace.HBM)


def traded(value, axis, turn):
    peers = lax.axis_size(axis)
    return lax.ppermute(value, axis, [(i, i ^ turn) for i in range(peers)])


def moved(value, axis, by):
    peers = lax.axis_size(axis)
    return lax.ppermute(value, axis, [(i, i + by) for i in range(peers - by)])


def local(
    x_in, bc_in, z_in, dt_raw, dt_bias, a_log, conv_x, conv_bc, conv_x_bias, conv_bc_bias,
    norm_weight,
):
    tokens, width = x_in.shape
    heads = dt_raw.shape[0]
    packed = width + LANES
    groups = width // LANES
    teams = lax.axis_size("seq") // TEAM
    hbm = pl.BlockSpec(memory_space=pltpu.MemorySpace.HBM)
    (rim,) = call(
        rim_kernel, [((RIM, width + 2 * STATE), bf16)], (), 2, in_specs=[hbm] * 2
    )(pinned(x_in), pinned(bc_in))
    rim = moved(rim, "seq", 1)
    xc, b_blk, c_blk, cum, late, state, weight, side, edge, *taps = call(
        early_kernel,
        [
            ((tokens, width), bf16),
            ((tokens, STATE), bf16),
            ((tokens, STATE), bf16),
            ((tokens, LANES), f32),
            ((COPIES, tokens), f32),
            ((STATE, width), f32),
            ((EDGE, LANES), f32),
            ((ROWS, LANES), bf16),
            ((EDGE, width + 2 * STATE), bf16),
            ((CONV, width), f32),
            ((CONV, 2 * STATE), f32),
            ((groups, LANES), f32),
            ((2, STATE), f32),
        ],
        [
            ((tokens, width), bf16),
            ((tokens, 2 * STATE), bf16),
            ((heads, tokens), f32),
            ((1, heads), f32),
            ((1, heads), f32),
            ((groups + 2, RIM + tokens, LANES), f32),
            ((tokens, width), bf16),
            ((LANES, LANES), f32),
        ],
        8 + groups // 2,
        cost(2 * tokens * width * STATE, tokens * width, 6 * tokens * width),
        in_specs=[hbm] * 9,
    )(
        *map(
            pinned,
            (
                x_in, bc_in, dt_raw, dt_bias[None, :], a_log[None, :], conv_x, conv_bc,
                conv_x_bias.reshape(groups, LANES), conv_bc_bias.reshape(2, STATE),
            ),
        )
    )
    x_edge, b_edge, c_edge, *mine = call(
        edge_kernel,
        [((EDGE, width), bf16), ((EDGE, STATE), bf16), ((EDGE, STATE), bf16)]
        + [((ROWS, packed), bf16)] * TEAM,
        [
            ((groups + 2, RIM + EDGE, LANES), f32),
            ((EDGE, width), bf16),
            ((STATE, width), bf16),
        ],
    )(rim, edge, *taps, weight, state, side)
    theirs = [mine[0]] + [traded(mine[turn], "seq", turn) for turn in range(1, TEAM)]
    inner, outer, c_blk = call(
        inner_kernel,
        [((tokens, width), f32)] * 2 + [((tokens, STATE), bf16)],
        (),
        0,
        cost(6 * tokens * tokens * width // 2, tokens * tokens * heads, 14 * tokens * width),
    )(xc, b_blk, c_blk, x_edge, b_edge, c_edge, cum, late, z_in)
    whole, team_local, lead = call(
        team_kernel,
        [
            ((ROWS, packed), bf16),
            ((TEAM, ROWS, width), f32),
            ((TEAM, ROWS // 2, LANES), f32),
        ],
        [((TEAM, ROWS, packed), bf16)],
    )(*theirs)
    before = traded(whole, "seq", TEAM) if teams == 2 else moved(whole, "seq", TEAM)
    reach = 1
    while reach < teams - 1:
        (before,) = call(merge_kernel, [((ROWS, packed), bf16)])(
            moved(before, "seq", reach * TEAM), before
        )
        reach *= 2
    before, inner, outer, c_blk = lax.optimization_barrier((before, inner, outer, c_blk))
    mine = call(spread_kernel, [((ROWS, width), bf16)] * TEAM)(before, team_local, lead)
    theirs = [mine[0]] + [traded(mine[turn], "seq", turn) for turn in range(1, TEAM)]
    gated, squares = call(
        outer_kernel,
        [((tokens, width), f32), ((1, tokens), f32)],
        [((STATE, width), bf16)],
    )(c_blk, *theirs, inner, outer)
    shares = lax.axis_size("head")
    sums = [squares] + [traded(squares, "head", turn) for turn in range(1, shares)]
    (y_out,) = call(
        functools.partial(norm_kernel, float(width * shares)),
        [((tokens, width), bf16)],
        [((tokens, width), bf16)],
        4,
        out_specs=[hbm],
    )(gated, norm_weight.reshape(groups, LANES), *sums)
    return y_out


def solution(mesh):
    placed = (
        P("seq", "head"),
        P("seq", None),
        P("seq", "head"),
        P("head", "seq"),
        P("head"),
        P("head"),
        P(None, "head"),
        P(),
        P("head"),
        P(),
        P("head"),
    )
    return jax.shard_map(
        local, mesh=mesh, in_specs=placed, out_specs=P("seq", "head"), check_vma=False
    )
```

```python
import functools

import jax
import jax.numpy as jnp
from jax import lax
from jax.experimental import pallas as pl
from jax.experimental.pallas import tpu as pltpu
from jax.sharding import PartitionSpec as P

HEADDIM = 64
STATE = 128
CONV = 4
LANES = 128
RIM = 8
EDGE = 16
PAST = CONV - 1
TAIL = 8
HIGH = 0
LOW = HIGH + PAST + 1
FIRST_B = LOW + PAST + 1
LAST_B = FIRST_B + PAST
LAST_C = LAST_B + PAST
NOTES = LAST_C + PAST
TEAM = 4
ROWS = STATE // TEAM
COPIES = 32


f32 = jnp.float32
bf16 = jnp.bfloat16


def params(mib=24):
    return pltpu.CompilerParams(vmem_limit_bytes=mib << 20)


def cost(flops, transcendentals, nbytes):
    return pl.CostEstimate(
        flops=flops, transcendentals=transcendentals, bytes_accessed=nbytes
    )


def group(index):
    return slice(index * LANES, (index + 1) * LANES)


def half_silu(half):
    return half + half * jnp.tanh(half)


def lower_half(shape):
    return lax.broadcasted_iota(jnp.int32, shape, 1) < HEADDIM


def two_heads(by_head, index):
    shape = (by_head.shape[0], LANES)
    first = jnp.broadcast_to(by_head[:, 2 * index : 2 * index + 1], shape)
    second = jnp.broadcast_to(by_head[:, 2 * index + 1 : 2 * index + 2], shape)
    return jnp.where(lower_half(shape), first, second)


def conv_group(padded, taps, bias, tokens):
    running = bias
    for offset in range(CONV):
        first = RIM - (CONV - 1) + offset
        running = running + taps[offset : offset + 1] * padded[first : first + tokens, :]
    return half_silu(running).astype(bf16)


def fetch(sources, targets, semaphores):
    copies = [
        pltpu.make_async_copy(source, target, semaphores.at[place])
        for place, (source, target) in enumerate(zip(sources, targets))
    ]
    for copy in copies:
        copy.start()
    return copies


def rim_kernel(x_ref, bc_ref, rim_ref, semaphores):
    tokens, width = x_ref.shape
    last = slice(tokens - RIM, tokens)
    copies = fetch(
        (x_ref.at[last, :], bc_ref.at[last, :]),
        (rim_ref.at[:, 0:width], rim_ref.at[:, width:]),
        semaphores,
    )
    for copy in copies:
        copy.wait()


def scan_decay(raw, bias, rate):
    tokens = raw.shape[1]
    blank = jnp.zeros((LANES - raw.shape[0], tokens), f32)
    shifted = jnp.concatenate([raw, blank], axis=0).T + bias
    step = jnp.maximum(shifted, 0.0) + jnp.log1p(jnp.exp(-jnp.abs(shifted)))
    log_decay = step * -jnp.exp(rate)
    causal = lax.broadcasted_iota(jnp.int32, (tokens, tokens), 0) >= (
        lax.broadcasted_iota(jnp.int32, (tokens, tokens), 1)
    )
    causal = causal.astype(bf16)
    cum = 0.0
    for _ in range(3):
        part = log_decay.astype(bf16)
        log_decay = log_decay - part.astype(f32)
        cum = cum + jnp.dot(causal, part, preferred_element_type=f32)
    return step, cum


def early_kernel(
    direct,
    x_hbm, bc_hbm, dt_hbm, bias_hbm, rate_hbm, tx_hbm, tb_hbm, bx_hbm, bb_hbm,
    xc_ref, b_ref, c_ref, cum_ref, late_ref, edge_ref, tx_ref, tb_ref, bx_ref, bb_ref, *refs,
):
    outs, scratch = refs[: TEAM if direct else 3], refs[TEAM if direct else 3 :]
    x_ref, bc_ref, dt_ref, bias_ref, rate_ref, padded, weighted, decay, tail, state = scratch[:-1]
    semaphores = scratch[-1]
    tokens, width = x_ref.shape
    groups = width // LANES
    chunks = width // (2 * LANES)
    small = fetch(
        (dt_hbm, bias_hbm, rate_hbm, bc_hbm, tb_hbm, bb_hbm, tx_hbm, bx_hbm),
        (dt_ref, bias_ref, rate_ref, bc_ref, tb_ref, bb_ref, tx_ref, bx_ref),
        semaphores,
    )
    large = fetch(
        [x_hbm.at[:, pl.ds(2 * LANES * place, 2 * LANES)] for place in range(chunks)],
        [x_ref.at[:, pl.ds(2 * LANES * place, 2 * LANES)] for place in range(chunks)],
        semaphores.at[pl.ds(len(small), chunks)],
    )
    for copy in small[0:3]:
        copy.wait()
    heads = dt_ref.shape[0]
    blank = jnp.zeros((1, LANES - heads), f32)
    step, cum = scan_decay(
        dt_ref[...],
        jnp.concatenate([bias_ref[...], blank], axis=1),
        jnp.concatenate([rate_ref[...], blank], axis=1),
    )
    cum_ref[...] = cum
    late_ref[...] = (cum - jnp.log(step)).T[0:COPIES, :]
    last = cum[tokens - 1 : tokens, :]
    weight = jnp.exp(last - cum) * step
    inside = lax.broadcasted_iota(jnp.int32, weight.shape, 0) >= (PAST if direct else EDGE)
    early_weight = weight[0:EDGE, :]
    weight = jnp.where(inside, weight, 0.0)

    def fill(place, source):
        padded[place, 0:RIM, :] = jnp.zeros((RIM, LANES), f32)
        padded[place, RIM:, :] = source.astype(f32)
        return padded.at[place]

    for copy in small[3:6]:
        copy.wait()
    b_pad = fill(0, bc_ref[:, 0:STATE])
    b_blk = conv_group(b_pad, 0.5 * tb_ref[:, 0:STATE], 0.5 * bb_ref[0:1, :], tokens)
    b_ref[...] = b_blk
    b_turned = b_blk.astype(f32).T.astype(bf16)
    c_pad = fill(1, bc_ref[:, STATE:])
    c_ref[...] = conv_group(c_pad, 0.5 * tb_ref[:, STATE:], 0.5 * bb_ref[1:2, :], tokens)
    edge_ref[:, width:] = bc_ref[0:EDGE, :]
    for copy in small[6:8]:
        copy.wait()
    for index in range(groups):
        part = group(index)
        if index % 2 == 0:
            large[index // 2].wait()
        x_pad = fill(2 + index, x_ref[:, part])
        x_blk = conv_group(
            x_pad, 0.5 * tx_ref[:, part], 0.5 * bx_ref[index : index + 1, :], tokens
        )
        xc_ref[:, part] = x_blk
        edge_ref[:, part] = x_ref[0:EDGE, part]
        weighted[:, part] = (x_blk.astype(f32) * two_heads(weight, index)).astype(bf16)
        if index % 2 == 1:
            both = slice((index - 1) * LANES, (index + 1) * LANES)
            state[:, both] = jnp.dot(b_turned, weighted[:, both], preferred_element_type=f32)

    if not direct:
        state_ref, weight_ref, side_ref = outs
        state_ref[...] = state[...]
        weight_ref[...] = early_weight
        decay[...] = jnp.broadcast_to(jnp.exp(last), (LANES, LANES)).T
        side = jnp.concatenate(
            [
                jnp.where(
                    lower_half((1, LANES)),
                    decay[2 * index : 2 * index + 1, :],
                    decay[2 * index + 1 : 2 * index + 2, :],
                )
                for index in range(groups)
            ]
            + [jnp.zeros((ROWS // 2 - groups, LANES), f32)],
            axis=0,
        )
        store_side(side_ref, 0, side)
        return
    tail[0:PAST, :] = x_ref[0:TAIL, :].astype(f32)[0:PAST]
    tail[PAST : 2 * PAST, :] = x_ref[tokens - TAIL :, :].astype(f32)[TAIL - PAST :]
    fine = jnp.concatenate([jnp.exp(last), early_weight[0:PAST]], axis=0)
    coarse = fine.astype(bf16).astype(f32)
    fine = fine - coarse
    first_bc = bc_ref[0:TAIL, :].astype(f32)
    last_bc = bc_ref[tokens - TAIL :, :].astype(f32)
    notes = [None] * NOTES
    for row in range(PAST + 1):
        notes[HIGH + row] = coarse[row : row + 1]
        notes[LOW + row] = fine[row : row + 1]
    for row in range(PAST):
        notes[FIRST_B + row] = first_bc[row : row + 1, 0:STATE]
        old = slice(TAIL - PAST + row, TAIL - PAST + row + 1)
        notes[LAST_B + row] = last_bc[old, 0:STATE]
        notes[LAST_C + row] = last_bc[old, STATE:]
    tail[2 * PAST : TAIL, :] = jnp.zeros((TAIL - 2 * PAST, width), f32)
    for note, row in enumerate(notes):
        line = 2 * PAST + note // groups
        tail[line : line + 1, group(note % groups)] = row
    slot = lax.rem(lax.axis_index("seq"), TEAM)
    for turn, out_ref in enumerate(outs):
        rows = pl.ds(pl.multiple_of((slot ^ turn) * ROWS, ROWS), ROWS)
        out_ref[0:ROWS, :] = state[rows, :].astype(bf16)
        out_ref[ROWS:, :] = tail[...].astype(bf16)


def noted(tail, note, count):
    groups = tail.shape[1] // LANES
    rows = []
    for index in range(note, note + count):
        line = 2 * PAST + index // groups
        rows.append(tail[line : line + 1, group(index % groups)])
    return jnp.concatenate(rows, axis=0)


def noted_weights(tail):
    return noted(tail, HIGH + 1, PAST) + noted(tail, LOW + 1, PAST)


def tall(rows, count):
    blank = jnp.zeros((count - rows.shape[0], rows.shape[1]), rows.dtype)
    return jnp.concatenate([rows, blank], axis=0)


def first_rows(pad, place, part, taps, bias):
    running = bias
    for offset in range(CONV):
        running = running + taps[offset : offset + 1] * pad[place, offset : offset + TAIL, part]
    return half_silu(running).astype(bf16)


def first_terms(pad_x, pad_b, weights, turned, weighted, slot, tx_ref, tb_ref, bx_ref, bb_ref):
    members, _, width = pad_x.shape
    b_first = jnp.concatenate(
        [
            first_rows(
                pad_b, k, slice(0, STATE), 0.5 * tb_ref[:, 0:STATE], 0.5 * bb_ref[0:1, :]
            ).astype(f32)
            for k in range(members)
        ],
        axis=0,
    )
    turned[...] = tall(b_first, STATE).T
    for index in range(width // LANES):
        part = group(index)
        x_first = jnp.concatenate(
            [
                first_rows(
                    pad_x, k, part, 0.5 * tx_ref[:, part], 0.5 * bx_ref[index : index + 1, :]
                ).astype(f32)
                for k in range(members)
            ],
            axis=0,
        )
        weighted[:, part] = (x_first * two_heads(weights, index)).astype(bf16)
    mine = turned[pl.ds(pl.multiple_of(slot * ROWS, ROWS), ROWS), 0 : members * TAIL]
    column = lax.broadcasted_iota(jnp.int32, mine.shape, 1) // TAIL
    return jnp.concatenate(
        [jnp.where(column == k, mine, 0.0) for k in range(members)], axis=0
    ).astype(bf16)


def join_kernel(
    own_ref, one_ref, two_ref, three_ref, tx_ref, tb_ref, bx_ref, bb_ref,
    whole_ref, local_ref, lead_ref, first_ref, rim_ref,
    buffer, pad_x, pad_b, turned, weighted, tail,
):
    width = local_ref.shape[2]
    groups = width // LANES
    place = lax.axis_index("seq")
    slot = lax.rem(place, TEAM)
    for turn, in_ref in enumerate((own_ref, one_ref, two_ref, three_ref)):
        buffer[slot ^ turn] = in_ref[...]
    weights, shrinks = [], []
    for k in range(TEAM):
        tail[k] = buffer[k, ROWS:, :].astype(f32)
        known = tail[k]
        pad_x[k, 2 * PAST :, :] = jnp.zeros((pad_x.shape[1] - 2 * PAST, width), f32)
        pad_b[k, 2 * PAST :, :] = jnp.zeros((pad_b.shape[1] - 2 * PAST, STATE), f32)
        if k == 0:
            pad_x[k, 0:PAST, :] = jnp.zeros((PAST, width), f32)
            pad_b[k, 0:PAST, :] = jnp.zeros((PAST, STATE), f32)
        else:
            older = tail[k - 1]
            pad_x[k, 0:PAST, :] = older[PAST : 2 * PAST]
            pad_b[k, 0:PAST, :] = noted(older, LAST_B, PAST)
        pad_x[k, PAST : 2 * PAST, :] = known[0:PAST]
        pad_b[k, PAST : 2 * PAST, :] = noted(known, FIRST_B, PAST)
        weight = noted_weights(known)
        if k == 0:
            weight = jnp.where(place < TEAM, weight, 0.0)
        weights.append(tall(weight, TAIL))
        shrinks.append(noted(known, HIGH, 1) + noted(known, LOW, 1))
    lhs = first_terms(
        pad_x, pad_b, jnp.concatenate(weights, axis=0), turned, weighted, slot,
        tx_ref, tb_ref, bx_ref, bb_ref,
    )
    one = jnp.ones((1, LANES), f32)
    leads, afters = [one], [one, one]
    for k in range(TEAM - 1):
        leads.append(leads[-1] * shrinks[k])
        if k > 0:
            afters.append(afters[-1] * shrinks[k])
    lead_ref[0] = tall(jnp.concatenate(leads, axis=0), TAIL)
    lead_ref[1] = tall(jnp.concatenate(afters, axis=0), TAIL)
    shrink = tall(jnp.concatenate(shrinks, axis=0), TAIL)
    for pair in range(groups // 2):
        both = slice(2 * pair * LANES, 2 * (pair + 1) * LANES)
        terms = jnp.dot(lhs, weighted[:, both], preferred_element_type=f32)
        for index in (2 * pair, 2 * pair + 1):
            part = group(index)
            term = terms[:, group(index % 2)]
            by_member = two_heads(shrink, index)
            held = jnp.zeros((ROWS, LANES), f32)
            for k in range(TEAM):
                local_ref[k, :, part] = held
                held = held * by_member[k : k + 1, :] + (
                    buffer[k, 0:ROWS, part].astype(f32) + term[k * ROWS : (k + 1) * ROWS]
                )
            whole_ref[0:ROWS, part] = held.astype(bf16)
    newest = tail[TEAM - 1]
    pass_on = tall(newest[PAST : 2 * PAST], TAIL)
    first_ref[...] = tail[0]
    tail[0] = pass_on
    for row in range(PAST):
        line = slice(PAST, PAST + 1)
        tail[0, line, group(row)] = noted(newest, LAST_B + row, 1)
        tail[0, line, group(PAST + row)] = noted(newest, LAST_C + row, 1)
    whole_ref[ROWS:, :] = tail[0].astype(bf16)
    older = buffer[jnp.maximum(slot - 1, 0), ROWS:, :].astype(f32)
    rim_ref[...] = jnp.zeros(rim_ref.shape, f32)
    rim_ref[RIM - PAST :, 0:width] = older[PAST : 2 * PAST]
    rim_ref[RIM - PAST :, width : width + STATE] = noted(older, LAST_B, PAST)
    rim_ref[RIM - PAST :, width + STATE :] = noted(older, LAST_C, PAST)


def share_kernel(
    before_ref, local_ref, lead_ref, first_ref, tx_ref, tb_ref, bx_ref, bb_ref,
    own_ref, one_ref, two_ref, three_ref,
    pad_x, pad_b, turned, weighted, terms,
):
    width = own_ref.shape[1]
    groups = width // LANES
    place = lax.axis_index("seq")
    slot = lax.rem(place, TEAM)
    later = place >= TEAM
    known = first_ref[...]
    older = before_ref[ROWS:, :].astype(f32)
    pad_x[0, 2 * PAST :, :] = jnp.zeros((pad_x.shape[1] - 2 * PAST, width), f32)
    pad_b[0, 2 * PAST :, :] = jnp.zeros((pad_b.shape[1] - 2 * PAST, STATE), f32)
    pad_x[0, 0:PAST, :] = older[0:PAST]
    pad_x[0, PAST : 2 * PAST, :] = known[0:PAST]
    for row in range(PAST):
        pad_b[0, row : row + 1, :] = older[PAST : PAST + 1, group(row)]
    pad_b[0, PAST : 2 * PAST, :] = noted(known, FIRST_B, PAST)
    weight = tall(jnp.where(later, noted_weights(known), 0.0), TAIL)
    lhs = first_terms(
        pad_x, pad_b, weight, turned, weighted, slot, tx_ref, tb_ref, bx_ref, bb_ref
    )
    terms[...] = jnp.dot(lhs, weighted[...], preferred_element_type=f32)
    for turn, out_ref in enumerate((own_ref, one_ref, two_ref, three_ref)):
        member = slot ^ turn
        lead = jnp.where(later, lead_ref[0, pl.ds(member, 1), :], 0.0)
        after = jnp.where(member > 0, lead_ref[1, pl.ds(member, 1), :], 0.0)
        both = tall(jnp.concatenate([lead, after], axis=0), TAIL)
        for index in range(groups):
            part = group(index)
            by_head = two_heads(both, index)
            out_ref[:, part] = (
                before_ref[0:ROWS, part].astype(f32) * by_head[0:1, :]
                + local_ref[member, :, part]
                + terms[:, part] * by_head[1:2, :]
            ).astype(bf16)


def edge_kernel(
    rim_ref, edge_ref, tx_ref, tb_ref, bx_ref, bb_ref, weight_ref, state_ref, side_ref,
    x_ref, b_ref, c_ref, own_ref, one_ref, two_ref, three_ref,
    padded, weighted, state,
):
    width = x_ref.shape[1]
    slot = lax.rem(lax.axis_index("seq"), TEAM)

    def fill(place, part):
        padded[place, 0:RIM, :] = rim_ref[:, part].astype(f32)
        padded[place, RIM:, :] = edge_ref[:, part].astype(f32)
        return padded.at[place]

    b_pad = fill(0, slice(width, width + STATE))
    b_blk = conv_group(b_pad, 0.5 * tb_ref[:, 0:STATE], 0.5 * bb_ref[0:1, :], EDGE)
    b_ref[...] = b_blk
    b_turned = b_blk.astype(f32).T.astype(bf16)
    c_pad = fill(1, slice(width + STATE, width + 2 * STATE))
    c_ref[...] = conv_group(c_pad, 0.5 * tb_ref[:, STATE:], 0.5 * bb_ref[1:2, :], EDGE)
    weight = weight_ref[...]
    for index in range(width // LANES):
        part = group(index)
        x_pad = fill(2 + index, part)
        x_blk = conv_group(
            x_pad, 0.5 * tx_ref[:, part], 0.5 * bx_ref[index : index + 1, :], EDGE
        )
        x_ref[:, part] = x_blk
        weighted[:, part] = (x_blk.astype(f32) * two_heads(weight, index)).astype(bf16)
        if index % 2 == 1:
            both = slice((index - 1) * LANES, (index + 1) * LANES)
            state[:, both] = (
                state_ref[:, both]
                + jnp.dot(b_turned, weighted[:, both], preferred_element_type=f32)
            ).astype(bf16)
    for turn, out_ref in enumerate((own_ref, one_ref, two_ref, three_ref)):
        rows = pl.ds(pl.multiple_of((slot ^ turn) * ROWS, ROWS), ROWS)
        out_ref[:, 0:width] = state[rows, :]
        out_ref[:, width:] = side_ref[...]


def decays(side):
    return side[0 : ROWS // 2, :].astype(f32) + side[ROWS // 2 :, :].astype(f32)


def store_side(out_ref, width, side):
    high = side.astype(bf16)
    out_ref[0 : ROWS // 2, width:] = high
    out_ref[ROWS // 2 :, width:] = (side - high.astype(f32)).astype(bf16)


def team_kernel(own_ref, one_ref, two_ref, three_ref, whole_ref, local_ref, lead_ref, buffer):
    width = local_ref.shape[2]
    groups = width // LANES
    slot = lax.rem(lax.axis_index("seq"), TEAM)
    for turn, in_ref in enumerate((own_ref, one_ref, two_ref, three_ref)):
        buffer[slot ^ turn] = in_ref[...]
    lead = jnp.ones((ROWS // 2, LANES), f32)
    held = [jnp.zeros((ROWS, LANES), f32)] * groups
    for member in range(TEAM):
        lead_ref[member] = lead
        own = decays(buffer[member, :, width:])
        for index in range(groups):
            part = group(index)
            local_ref[member, :, part] = held[index]
            held[index] = held[index] * own[index : index + 1, :] + (
                buffer[member, :, part].astype(f32)
            )
        lead = lead * own
    for index in range(groups):
        whole_ref[:, group(index)] = held[index].astype(bf16)
    store_side(whole_ref, width, lead)


def merge_kernel(far_ref, near_ref, out_ref):
    width = out_ref.shape[1] - LANES
    near = decays(near_ref[:, width:])
    for index in range(width // LANES):
        part = group(index)
        out_ref[:, part] = (
            far_ref[:, part].astype(f32) * near[index : index + 1, :]
            + near_ref[:, part].astype(f32)
        ).astype(bf16)
    store_side(out_ref, width, near * decays(far_ref[:, width:]))


def spread_kernel(before_ref, local_ref, lead_ref, own_ref, one_ref, two_ref, three_ref):
    width = own_ref.shape[1]
    place = lax.axis_index("seq")
    slot = lax.rem(place, TEAM)
    for turn, out_ref in enumerate((own_ref, one_ref, two_ref, three_ref)):
        member = slot ^ turn
        lead = jnp.where(place >= TEAM, lead_ref[member], 0.0)
        for index in range(width // LANES):
            part = group(index)
            out_ref[:, part] = (
                before_ref[:, part].astype(f32) * lead[index : index + 1, :]
                + local_ref[member, :, part]
            ).astype(bf16)


def repaired(rim_ref, before_ref, edge_ref, tx_ref, tb_ref, bx_ref, bb_ref, padded, x_ref, b_ref, c_ref):
    width = x_ref.shape[1]
    place = lax.axis_index("seq")
    slot = lax.rem(place, TEAM)
    older = before_ref[ROWS:, :].astype(f32)
    passed = older[PAST : PAST + 1, :]

    def fill(at, part, across):
        rim = jnp.where(slot > 0, rim_ref[RIM - PAST :, part], jnp.where(place > 0, across, 0.0))
        padded[at, 0:RIM, :] = jnp.concatenate([jnp.zeros((RIM - PAST, LANES), f32), rim], axis=0)
        padded[at, RIM:, :] = edge_ref[:, part].astype(f32)
        return padded.at[at]

    def lines(start):
        return jnp.concatenate(
            [passed[:, group(start + row)] for row in range(PAST)], axis=0
        )

    b_pad = fill(0, slice(width, width + STATE), lines(0))
    b_ref[...] = conv_group(b_pad, 0.5 * tb_ref[:, 0:STATE], 0.5 * bb_ref[0:1, :], EDGE)
    c_pad = fill(1, slice(width + STATE, width + 2 * STATE), lines(PAST))
    c_ref[...] = conv_group(c_pad, 0.5 * tb_ref[:, STATE:], 0.5 * bb_ref[1:2, :], EDGE)
    for index in range(width // LANES):
        part = group(index)
        x_pad = fill(2 + index, part, older[0:PAST, part])
        x_ref[:, part] = conv_group(
            x_pad, 0.5 * tx_ref[:, part], 0.5 * bx_ref[index : index + 1, :], EDGE
        )


def repaired_inner_kernel(
    xc_ref, b_part, c_part, cum_ref, late_ref, z_ref,
    rim_ref, before_ref, edge_ref, tx_ref, tb_ref, bx_ref, bb_ref,
    inner_ref, outer_ref, c_ref,
    padded, x_edge, b_edge, c_edge,
):
    repaired(
        rim_ref, before_ref, edge_ref, tx_ref, tb_ref, bx_ref, bb_ref,
        padded, x_edge, b_edge, c_edge,
    )
    inner_kernel(
        xc_ref, b_part, c_part, x_edge, b_edge, c_edge, cum_ref, late_ref, z_ref,
        inner_ref, outer_ref, c_ref,
    )


def inner_kernel(
    xc_ref, b_part, c_part, x_edge, b_edge, c_edge, cum_ref, late_ref, z_ref,
    inner_ref, outer_ref, c_ref,
):
    tokens, width = xc_ref.shape
    half = tokens // 2
    b_blk = jnp.concatenate([b_edge[...], b_part[EDGE:, :]], axis=0)
    c_blk = jnp.concatenate([c_edge[...], c_part[EDGE:, :]], axis=0)
    c_ref[...] = c_blk
    scores = lax.dot_general(
        c_blk, b_blk, (((1,), (1,)), ((), ())), preferred_element_type=f32
    )
    causal = lax.broadcasted_iota(jnp.int32, (half, half), 0) >= (
        lax.broadcasted_iota(jnp.int32, (half, half), 1)
    )
    cum = cum_ref[...]
    grown = jnp.exp(cum)
    first = lower_half((half, LANES))
    for index in range(width // LANES):
        part = group(index)
        near, cross, far = [], [], []
        for head in (2 * index, 2 * index + 1):
            upto = jnp.broadcast_to(cum[:, head : head + 1], (tokens, half))
            early = late_ref[head : head + 1, 0:half]
            later = late_ref[head : head + 1, half:]
            near.append(
                jnp.exp(jnp.where(causal, upto[:half] - early, -1e30)) * scores[:half, :half]
            )
            cross.append(jnp.exp(upto[half:] - early) * scores[half:, :half])
            far.append(
                jnp.exp(jnp.where(causal, upto[half:] - later, -1e30)) * scores[half:, half:]
            )
        x_early = jnp.concatenate([x_edge[:, part], xc_ref[EDGE:half, part]], axis=0)
        x_later = xc_ref[half:, part]
        zero = jnp.zeros_like(x_early)
        x_early = jnp.concatenate(
            [jnp.where(first, x_early, zero), jnp.where(first, zero, x_early)], axis=0
        )
        x_later = jnp.concatenate(
            [jnp.where(first, x_later, zero), jnp.where(first, zero, x_later)], axis=0
        )

        def times(mixing, x_blk):
            return jnp.dot(
                jnp.concatenate(mixing, axis=1).astype(bf16), x_blk, preferred_element_type=f32
            )

        y_blk = jnp.concatenate(
            [times(near, x_early), times(cross, x_early) + times(far, x_later)], axis=0
        )
        gate = half_silu(0.5 * z_ref[:, part].astype(f32))
        inner_ref[:, part] = y_blk * gate
        outer_ref[:, part] = two_heads(grown, index) * gate


def outer_kernel(
    c_ref, own_ref, one_ref, two_ref, three_ref, inner_ref, outer_ref, gated_ref, sum_ref, state
):
    tokens, width = inner_ref.shape
    slot = lax.rem(lax.axis_index("seq"), TEAM)
    for turn, in_ref in enumerate((own_ref, one_ref, two_ref, three_ref)):
        rows = pl.ds(pl.multiple_of((slot ^ turn) * ROWS, ROWS), ROWS)
        state[rows, :] = in_ref[...]
    c_blk = c_ref[...]
    total = jnp.zeros((tokens, LANES), f32)
    for index in range(width // LANES):
        part = group(index)
        y_blk = jnp.dot(c_blk, state[:, part], preferred_element_type=f32)
        gated = inner_ref[:, part] + y_blk * outer_ref[:, part]
        gated_ref[:, part] = gated
        total = total + gated * gated
    sum_ref[...] = jnp.sum(total.T, axis=0, keepdims=True)


def norm_kernel(channels, gated_ref, gain_ref, *refs):
    out_hbm, out_ref, semaphores = refs[-3:]
    whole = refs[0][...]
    for other in refs[1:-3]:
        whole = whole + other[...]
    inv_rms = lax.rsqrt(whole / channels + 1e-05)
    tokens, width = gated_ref.shape
    inv_rms = jnp.broadcast_to(inv_rms, (LANES, tokens)).T
    pieces = semaphores.shape[0]
    rows = tokens // pieces
    copies = []
    for piece in range(pieces):
        block = slice(piece * rows, (piece + 1) * rows)
        for index in range(width // LANES):
            part = group(index)
            out_ref[block, part] = (
                gated_ref[block, part] * inv_rms[block, :] * gain_ref[index : index + 1, :]
            ).astype(bf16)
        copy = pltpu.make_async_copy(
            out_ref.at[block, :], out_hbm.at[block, :], semaphores.at[piece]
        )
        copy.start()
        copies.append(copy)
    for copy in copies:
        copy.wait()


def call(kernel, outs, scratch=(), copies=0, estimate=None, **kw):
    return pl.pallas_call(
        kernel,
        out_shape=[jax.ShapeDtypeStruct(shape, kind) for shape, kind in outs],
        scratch_shapes=[pltpu.VMEM(shape, kind) for shape, kind in scratch]
        + [pltpu.SemaphoreType.DMA((copies,))] * (copies > 0),
        compiler_params=params(),
        cost_estimate=estimate,
        **kw,
    )


def pinned(value):
    return pltpu.with_memory_space_constraint(value, pltpu.MemorySpace.HBM)


def traded(value, axis, turn):
    peers = lax.axis_size(axis)
    return lax.ppermute(value, axis, [(i, i ^ turn) for i in range(peers)])


def moved(value, axis, by):
    peers = lax.axis_size(axis)
    return lax.ppermute(value, axis, [(i, i + by) for i in range(peers - by)])


def local(
    x_in, bc_in, z_in, dt_raw, dt_bias, a_log, conv_x, conv_bc, conv_x_bias, conv_bc_bias,
    norm_weight,
):
    tokens, width = x_in.shape
    heads = dt_raw.shape[0]
    packed = width + LANES
    groups = width // LANES
    teams = lax.axis_size("seq") // TEAM
    hbm = pl.BlockSpec(memory_space=pltpu.MemorySpace.HBM)
    wide = width + 2 * STATE
    direct = teams == 2 and NOTES <= (TAIL - 2 * PAST) * groups
    inner_cost = cost(
        6 * tokens * tokens * width // 2, tokens * tokens * heads, 14 * tokens * width
    )
    inner_outs = [((tokens, width), f32)] * 2 + [((tokens, STATE), bf16)]
    pads = ((groups + 2, RIM + EDGE, LANES), f32)
    if direct:
        outs = [((ROWS + TAIL, width), bf16)] * TEAM
    else:
        (rim,) = call(
            rim_kernel, [((RIM, wide), bf16)], (), 2, in_specs=[hbm] * 2
        )(pinned(x_in), pinned(bc_in))
        rim = moved(rim, "seq", 1)
        outs = [((STATE, width), f32), ((EDGE, LANES), f32), ((ROWS, LANES), bf16)]
    xc, b_blk, c_blk, cum, late, edge, *rest = call(
        functools.partial(early_kernel, direct),
        [
            ((tokens, width), bf16),
            ((tokens, STATE), bf16),
            ((tokens, STATE), bf16),
            ((tokens, LANES), f32),
            ((COPIES, tokens), f32),
            ((EDGE, wide), bf16),
            ((CONV, width), f32),
            ((CONV, 2 * STATE), f32),
            ((groups, LANES), f32),
            ((2, STATE), f32),
        ]
        + outs,
        [
            ((tokens, width), bf16),
            ((tokens, 2 * STATE), bf16),
            ((heads, tokens), f32),
            ((1, heads), f32),
            ((1, heads), f32),
            ((groups + 2, RIM + tokens, LANES), f32),
            ((tokens, width), bf16),
            ((LANES, LANES), f32),
            ((TAIL, width), f32),
            ((STATE, width), f32),
        ],
        8 + groups // 2,
        cost(2 * tokens * width * STATE, tokens * width, 6 * tokens * width),
        in_specs=[hbm] * 9,
    )(
        *map(
            pinned,
            (
                x_in, bc_in, dt_raw, dt_bias[None, :], a_log[None, :], conv_x, conv_bc,
                conv_x_bias.reshape(groups, LANES), conv_bc_bias.reshape(2, STATE),
            ),
        )
    )
    taps, rest = rest[0:4], rest[4:]
    if direct:
        theirs = [rest[0]] + [traded(rest[turn], "seq", turn) for turn in range(1, TEAM)]
        whole, team_local, lead, first, rim = call(
            join_kernel,
            [
                ((ROWS + TAIL, width), bf16),
                ((TEAM, ROWS, width), f32),
                ((2, TAIL, LANES), f32),
                ((TAIL, width), f32),
                ((RIM, wide), f32),
            ],
            [
                ((TEAM, ROWS + TAIL, width), bf16),
                ((TEAM, 2 * TAIL, width), f32),
                ((TEAM, 2 * TAIL, STATE), f32),
                ((STATE, STATE), f32),
                ((TEAM * TAIL, width), bf16),
                ((TEAM, TAIL, width), f32),
            ],
        )(*theirs, *taps)
        before = traded(whole, "seq", TEAM)
        mine = call(
            share_kernel,
            [((ROWS, width), bf16)] * TEAM,
            [
                ((1, 2 * TAIL, width), f32),
                ((1, 2 * TAIL, STATE), f32),
                ((STATE, STATE), f32),
                ((TAIL, width), bf16),
                ((ROWS, width), f32),
            ],
        )(before, team_local, lead, first, *taps)
        inner, outer, c_blk = call(
            repaired_inner_kernel,
            inner_outs,
            [pads, ((EDGE, width), bf16), ((EDGE, STATE), bf16), ((EDGE, STATE), bf16)],
            0,
            inner_cost,
        )(xc, b_blk, c_blk, cum, late, z_in, rim, before, edge, *taps)
    else:
        state, weight, side = rest
        x_edge, b_edge, c_edge, *mine = call(
            edge_kernel,
            [((EDGE, width), bf16), ((EDGE, STATE), bf16), ((EDGE, STATE), bf16)]
            + [((ROWS, packed), bf16)] * TEAM,
            [pads, ((EDGE, width), bf16), ((STATE, width), bf16)],
        )(rim, edge, *taps, weight, state, side)
        theirs = [mine[0]] + [traded(mine[turn], "seq", turn) for turn in range(1, TEAM)]
        inner, outer, c_blk = call(inner_kernel, inner_outs, (), 0, inner_cost)(
            xc, b_blk, c_blk, x_edge, b_edge, c_edge, cum, late, z_in
        )
        whole, team_local, lead = call(
            team_kernel,
            [
                ((ROWS, packed), bf16),
                ((TEAM, ROWS, width), f32),
                ((TEAM, ROWS // 2, LANES), f32),
            ],
            [((TEAM, ROWS, packed), bf16)],
        )(*theirs)
        before = moved(whole, "seq", TEAM)
        reach = 1
        while reach < teams - 1:
            (before,) = call(merge_kernel, [((ROWS, packed), bf16)])(
                moved(before, "seq", reach * TEAM), before
            )
            reach *= 2
        mine = call(spread_kernel, [((ROWS, width), bf16)] * TEAM)(before, team_local, lead)
    theirs = [mine[0]] + [traded(mine[turn], "seq", turn) for turn in range(1, TEAM)]
    gated, squares = call(
        outer_kernel,
        [((tokens, width), f32), ((1, tokens), f32)],
        [((STATE, width), bf16)],
    )(c_blk, *theirs, inner, outer)
    shares = lax.axis_size("head")
    sums = [squares] + [traded(squares, "head", turn) for turn in range(1, shares)]
    (y_out,) = call(
        functools.partial(norm_kernel, float(width * shares)),
        [((tokens, width), bf16)],
        [((tokens, width), bf16)],
        4,
        out_specs=[hbm],
    )(gated, norm_weight.reshape(groups, LANES), *sums)
    return y_out


def solution(mesh):
    placed = (
        P("seq", "head"),
        P("seq", None),
        P("seq", "head"),
        P("head", "seq"),
        P("head"),
        P("head"),
        P(None, "head"),
        P(),
        P("head"),
        P(),
        P("head"),
    )
    return jax.shard_map(
        local, mesh=mesh, in_specs=placed, out_specs=P("seq", "head"), check_vma=False
    )
```
